128 devices in a mesh: alpha: 16 (over z, y), beta: 8 (over x, core).
Axes of the slice: x: 4, y: 4, z: 4, core: 2. Of those that a mesh axis runs over, the one named last changes fastest.
Arguments:
- ci_vector: float32 [2048, 2048], P('alpha', 'beta'), may hold values from -6 to 6
- one_body: float32 [102], replicated, may hold values from -1 to 1
- pair_integrals: bfloat16 [102, 102], replicated, may hold values from -0.15625 to 0.15625
- beta_target: int32 [40, 2048], P(None, 'beta'), may hold values from 0 to 2047
- beta_pair: int32 [40, 2048], P(None, 'beta'), may hold values from 0 to 101
- beta_sign: int32 [40, 2048], P(None, 'beta'), may hold values 0 or 1
- alpha_target: int32 [40, 2048], P(None, 'alpha'), may hold values from 0 to 2047
- alpha_pair: int32 [40, 2048], P(None, 'alpha'), may hold values from 0 to 101
- alpha_sign: int32 [40, 2048], P(None, 'alpha'), may hold values 0 or 1
Outputs:
- sigma_vector: float32 [2048, 2048], P('alpha', 'beta')
The draws below stay inside these ranges and needn't reach their ends.
All inputs are finite; a program needn't handle non-finite values. No bound on the sum of `beta_sign` or of `alpha_sign` on one device may be relied on, other than what follows from the above.
Results may differ from the reference program's by a relative error of at most 0.0035.
Values may be sent and summed in bfloat16 or wider, within the bound.
A program may use at most 128 MiB of HBM per device.

```python
import jax
import jax.numpy as jnp
from jax import lax

NP = 102
NEXC = 40
NA = 2048
NB = 2048


def set_ends(result, stream_key, low, high):
    longest = result.shape.index(max(result.shape))
    spots = []
    for shift in (0, 1):
        where = [jax.random.randint(jax.random.fold_in(stream_key, axis), (), 0, length) for axis, length in enumerate(result.shape)]
        where[longest] = (where[longest] + shift) % result.shape[longest]
        spots.append(tuple(where))
    return result.at[spots[0]].set(low).at[spots[1]].set(high)


def steps_of(key, extent, shards, smallest, top_value):
    loudness, own = 1.0, jax.random.fold_in(key, 6)
    for position, blocks in shards:
        steps = jnp.exp(jax.random.uniform(jax.random.fold_in(own, position), (blocks,), jnp.float32, smallest / len(shards), top_value / len(shards)))
        loudness = loudness * jnp.repeat(steps, extent[position] // blocks).reshape([-1 if axis == position else 1 for axis in range(len(extent))])
    return loudness


def gaussian(stream_key, extent, width, most, split=(), kind=jnp.bfloat16):
    array = width * jax.random.normal(stream_key, extent, jnp.float32)
    if split:
        array = array * steps_of(stream_key, extent, split, -0.22, 0.18)
    return jnp.clip(array, -most, most).astype(kind)


def setup_inputs(seed: int = 0) -> dict:
    key_list = jax.random.split(jax.random.key(seed), 10)
    return {
        "ci_vector": gaussian(key_list[0], (NA, NB), 1.0, 6.0, ((0, 16), (1, 8)), jnp.float32),
        "one_body": gaussian(key_list[1], (NP,), NEXC ** -0.5, 1.0, (), jnp.float32),
        "pair_integrals": gaussian(key_list[2], (NP, NP), (NEXC * NEXC) ** -0.5, 0.15625),
        "beta_target": set_ends(jax.random.randint(key_list[3], (NEXC, NB), 0, NB), jax.random.fold_in(key_list[3], 1), 0, NB - 1).astype(jnp.int32),
        "beta_pair": set_ends(jax.random.randint(key_list[4], (NEXC, NB), 0, NP), jax.random.fold_in(key_list[4], 1), 0, NP - 1).astype(jnp.int32),
        "beta_sign": set_ends((jax.random.randint(key_list[5], (NEXC, NB), 0, 2) < 1).astype(jnp.int32), jax.random.fold_in(key_list[5], 1), 0, 1),
        "alpha_target": set_ends(jax.random.randint(key_list[6], (NEXC, NA), 0, NA), jax.random.fold_in(key_list[6], 1), 0, NA - 1).astype(jnp.int32),
        "alpha_pair": set_ends(jax.random.randint(key_list[7], (NEXC, NA), 0, NP), jax.random.fold_in(key_list[7], 1), 0, NP - 1).astype(jnp.int32),
        "alpha_sign": set_ends((jax.random.randint(key_list[8], (NEXC, NA), 0, 2) < 1).astype(jnp.int32), jax.random.fold_in(key_list[8], 1), 0, 1),
    }


precise = lax.Precision.HIGHEST


def reference(ci_vector, one_body, pair_integrals, beta_target, beta_pair, beta_sign, alpha_target, alpha_pair, alpha_sign):
    civec_bf = ci_vector.astype(jnp.bfloat16)
    civec_up = lax.optimization_barrier(civec_bf).astype(jnp.float32)
    pair_ids = jnp.arange(NP, dtype=jnp.int32)
    beta_hot = ((2 * beta_sign - 1)[:, :, None] * (beta_pair[:, :, None] == pair_ids).astype(jnp.int32)).astype(jnp.float32)
    alpha_hot = ((2 * alpha_sign - 1)[:, :, None] * (alpha_pair[:, :, None] == pair_ids).astype(jnp.int32)).astype(jnp.float32)
    alpha_level = jnp.einsum("eaq,q->ea", alpha_hot, one_body, precision=precise)
    integrals = pair_integrals.astype(jnp.float32)
    block_rows = 32

    def accumulate(sigma_out, block_index):
        offset = block_index * block_rows
        rows_here = lax.dynamic_slice_in_dim(civec_up, offset, block_rows, 0)
        picked = jnp.take(rows_here, beta_target, axis=1)
        density = jnp.einsum("aei,eip->pai", picked, beta_hot, precision=precise)
        same_beta = jnp.einsum("p,pai->ai", one_body, density, precision=precise)
        density_bf = lax.optimization_barrier(density.astype(jnp.bfloat16)).astype(jnp.float32)
        mixed = jnp.einsum("qp,pai->qai", integrals, density_bf, precision=precise)
        mixed_bf = lax.optimization_barrier(mixed.astype(jnp.bfloat16)).astype(jnp.float32)
        hot_rows = lax.dynamic_slice_in_dim(alpha_hot, offset, block_rows, 1)
        lifted = jnp.einsum("eaq,qai->aei", hot_rows, mixed_bf, precision=precise)
        level_rows = lax.dynamic_slice_in_dim(alpha_level, offset, block_rows, 1)
        lifted = lifted + level_rows.T[:, :, None] * rows_here[:, None, :]
        targets = lax.dynamic_slice_in_dim(alpha_target, offset, block_rows, 1)
        sigma_out = sigma_out.at[targets.T.reshape(-1)].add(lifted.reshape(-1, NB))
        current = lax.dynamic_slice_in_dim(sigma_out, offset, block_rows, 0)
        sigma_out = lax.dynamic_update_slice_in_dim(sigma_out, current + same_beta, offset, 0)
        return sigma_out, None

    sigma_out, unused = lax.scan(accumulate, jnp.zeros((NA, NB), jnp.float32), jnp.arange(NA // block_rows, dtype=jnp.int32))
    return sigma_out
```

```python
import functools

import jax
import jax.numpy as jnp
from jax import lax
from jax.experimental import pallas as pl
from jax.experimental.pallas import tpu as pltpu
from jax.sharding import PartitionSpec as P

BF = jnp.bfloat16
F32 = jnp.float32
NT = (((1,), (1,)), ((), ()))
TN = (((0,), (0,)), ((), ()))
LANES = 128
WIDE = 512
PICK_UNROLL = 2
DENS_UNROLL = 8


def iota(shape, dim):
    return lax.broadcasted_iota(jnp.int32, shape, dim)


def compute_kernel(
    hi_lane,
    rows_ref,
    one_ref,
    pair_ref,
    bt_ref,
    bp_ref,
    bs_ref,
    at_ref,
    ap_ref,
    as_ref,
    partial_ref,
    same_ref,
    code_ref,
    turned_ref,
    group_ref,
    dens_ref,
    sv_ref,
    lift_ref,
    lift_bf_ref,
    hot_ref,
    wide_ref,
    picked_ref,
):
    blocks, rows, cols = rows_ref.shape
    excits = bt_ref.shape[0]
    slots = excits + 2
    per_group = LANES // slots
    groups = group_ref.shape[0]
    used_groups = -(-cols // per_group)
    me_beta = lax.axis_index("beta")

    code_ref[...] = jnp.zeros_like(code_ref)
    listed = bt_ref[...] + 2048 * bp_ref[...] + (1 << 18) * bs_ref[...]
    code_ref[0:excits, :] = listed.astype(F32)
    own = me_beta * cols + iota((8, cols), 1)
    extra = iota((8, cols), 0)
    own = jnp.where(extra < 2, own + 2048 * (hi_lane + extra) + (1 << 18), 0)
    code_ref[excits : excits + 8, :] = own.astype(F32)
    turned_ref[...] = jnp.zeros_like(turned_ref)
    turned_ref[0:cols, :] = code_ref[...].T
    grouped = turned_ref[pl.ds(0, groups, stride=per_group), :]
    for t in range(1, per_group):
        shifted = turned_ref[pl.ds(t, groups, stride=per_group), :]
        grouped = grouped + pltpu.roll(shifted, t * slots, 1)
    group_ref[...] = grouped.astype(jnp.int32)

    one_row = one_ref[...]
    one_hi = one_row.astype(BF).astype(F32)
    one_lo = one_row - one_hi
    one_two = jnp.concatenate([one_hi, one_lo, jnp.zeros((6, LANES), F32)], axis=0)
    one_cols = jnp.concatenate([one_two, jnp.zeros((LANES - 8, LANES), F32)], axis=0).T
    lane = iota((LANES, LANES), 1)
    table = pair_ref[...].astype(F32)
    table = jnp.where(lane == hi_lane, one_cols[:, 0:1], table)
    table = jnp.where(lane == hi_lane + 1, one_cols[:, 1:2], table)
    table = table.astype(BF)

    def sv_step(e, carry):
        which = ap_ref[pl.ds(e, 1), :]
        sign = (2 * as_ref[pl.ds(e, 1), :] - 1).astype(F32)
        hot = jnp.where(iota((LANES, rows), 0) == which, sign, 0.0).astype(BF)
        sv = lax.dot_general(hot, table, TN, preferred_element_type=F32)
        sv_ref[pl.ds(pl.multiple_of(e * rows, rows), rows), :] = sv
        return carry

    lax.fori_loop(0, excits, sv_step, 0, unroll=8)
    sv_ref[excits * rows :, :] = jnp.zeros(((48 - excits) * rows, LANES), F32)
    sv_ref[excits * rows : (excits + 1) * rows, :] = jnp.broadcast_to(one_hi, (rows, LANES))
    sv_ref[(excits + 1) * rows : (excits + 2) * rows, :] = jnp.broadcast_to(one_lo, (rows, LANES))

    wide = wide_ref.shape[1]
    parts = blocks * cols // wide
    joined = wide // cols
    for m in range(blocks):
        wide_ref[
            (m // joined) * rows : (m // joined + 1) * rows,
            (m % joined) * cols : (m % joined + 1) * cols,
        ] = rows_ref[m]
    lane_row = iota((1, LANES), 1)
    lane_slot = lane_row // slots

    def pick_step(step, carry):
        coded = [group_ref[pl.ds(2 * step + u, 1), :] for u in range(2)]
        code = jnp.concatenate(coded, axis=1)
        target = jnp.bitwise_and(code, 2047)
        low = jnp.bitwise_and(target, wide - 1)
        block = target // wide
        sign = (2 * lax.shift_right_logical(code, 18) - 1).astype(F32)
        pick = jnp.where(iota((wide, 2 * LANES), 0) == low, sign, 0.0).astype(BF)
        found = jnp.dot(wide_ref[...], pick, preferred_element_type=F32)
        picked = found[0:rows]
        for m in range(1, parts):
            picked = jnp.where(block == m, found[m * rows : (m + 1) * rows], picked)
        picked = picked.astype(BF)
        for u in range(2):
            picked_ref[2 * step + u] = picked[:, u * LANES : (u + 1) * LANES]
        return carry

    lax.fori_loop(0, used_groups // 2, pick_step, 0, unroll=PICK_UNROLL)

    def density_step(g, carry):
        code = group_ref[pl.ds(g, 1), :]
        pair = jnp.bitwise_and(lax.shift_right_logical(code, 11), 127)
        goal = jnp.where(lane_slot < per_group, lane_slot * LANES + pair, -1)
        spots = iota((per_group * LANES, LANES), 0) == goal
        hot = jnp.where(spots, 1.0, 0.0).astype(BF)
        dens = lax.dot_general(picked_ref[g], hot, NT, preferred_element_type=F32)
        for t in range(per_group):
            base = (per_group * g + t) * rows
            dens_ref[pl.ds(pl.multiple_of(base, rows), rows), :] = dens[
                :, t * LANES : (t + 1) * LANES
            ]
        return carry

    lax.fori_loop(0, used_groups, density_step, 0, unroll=DENS_UNROLL)

    def lift_step(a, carry):
        weights = sv_ref[pl.ds(a, 48, stride=rows), :].astype(BF)
        dens = dens_ref[pl.ds(a, cols, stride=rows), :].astype(BF)
        out = lax.dot_general(weights, dens, NT, preferred_element_type=F32)
        for half in range(2):
            lift_ref[half, pl.ds(a, 48, stride=rows), :] = out[:, half * LANES : (half + 1) * LANES]
        return carry

    lax.fori_loop(0, rows, lift_step, 0, unroll=8)
    for half in range(2):
        at_half = slice(half * LANES, (half + 1) * LANES)
        same_ref[:, at_half] = (
            lift_ref[half, excits * rows : (excits + 1) * rows, :]
            + lift_ref[half, (excits + 1) * rows : (excits + 2) * rows, :]
        )
        lift_bf_ref[:, at_half] = lift_ref[half, 0 : excits * rows, :].astype(BF)

    tall = hot_ref.shape[0]

    def spread_step(d, carry):
        def hot_step(e, inner):
            goal = at_ref[pl.ds(e, 1), :] - d * tall
            hot = jnp.where(iota((tall, rows), 0) == goal, 1.0, 0.0).astype(BF)
            hot_ref[:, pl.ds(pl.multiple_of(e * rows, rows), rows)] = hot
            return inner

        lax.fori_loop(0, excits, hot_step, 0)
        out = jnp.dot(hot_ref[...], lift_bf_ref[...], preferred_element_type=F32)
        partial_ref[pl.ds(pl.multiple_of(d * tall, tall), tall), :] = out.astype(BF)
        return carry

    lax.fori_loop(0, partial_ref.shape[0] // tall, spread_step, 0)


def local_part(rows_whole, one_body, pair_integrals, bt, bp, bs, at, ap, asg, total_alpha):
    blocks, rows, cols = rows_whole.shape
    pairs = one_body.shape[0]
    excits = bt.shape[0]
    one_row = jnp.pad(one_body, (0, LANES - pairs)).reshape(1, LANES)
    table = jnp.pad(pair_integrals, ((0, LANES - pairs), (0, LANES - pairs)))
    per_group = LANES // (excits + 2)
    used = -(-cols // per_group)
    groups = -(-used // 8) * 8
    vmem = pl.BlockSpec(memory_space=pltpu.VMEM)
    return pl.pallas_call(
        functools.partial(compute_kernel, pairs),
        out_shape=(
            jax.ShapeDtypeStruct((total_alpha, cols), BF),
            jax.ShapeDtypeStruct((rows, cols), F32),
        ),
        in_specs=[vmem] * 9,
        out_specs=(vmem, vmem),
        scratch_shapes=[
            pltpu.VMEM((LANES, cols), F32),
            pltpu.VMEM((groups * per_group, LANES), F32),
            pltpu.VMEM((groups, LANES), jnp.int32),
            pltpu.VMEM((groups * per_group * rows, LANES), F32),
            pltpu.VMEM((48 * rows, LANES), F32),
            pltpu.VMEM((2, 48 * rows, LANES), F32),
            pltpu.VMEM((excits * rows, cols), BF),
            pltpu.VMEM((512, excits * rows), BF),
            pltpu.VMEM((blocks * rows * cols // WIDE, WIDE), BF),
            pltpu.VMEM((groups, rows, LANES), BF),
        ],
        compiler_params=pltpu.CompilerParams(vmem_limit_bytes=56 * 2**20),
    )(rows_whole, one_row, table, bt, bp, bs, at, ap, asg)


def sent_to_all(value, axis):
    copies = jnp.broadcast_to(value, (lax.axis_size(axis), *value.shape))
    return lax.all_to_all(copies, axis, split_axis=0, concat_axis=0, tiled=True)


def shards(
    ci_vector,
    one_body,
    pair_integrals,
    beta_target,
    beta_pair,
    beta_sign,
    alpha_target,
    alpha_pair,
    alpha_sign,
):
    alpha_count, beta_count = ci_vector.shape
    alpha_devices = lax.axis_size("alpha")
    rows_whole = sent_to_all(ci_vector.astype(BF), "beta")
    partial, same_beta = local_part(
        rows_whole,
        one_body,
        pair_integrals,
        beta_target,
        beta_pair,
        beta_sign,
        alpha_target,
        alpha_pair,
        alpha_sign,
        alpha_count * alpha_devices,
    )
    partial = partial.reshape(alpha_devices, alpha_count, beta_count)
    arrived = lax.all_to_all(partial, "alpha", split_axis=0, concat_axis=0, tiled=True)
    return arrived.astype(F32).sum(axis=0) + same_beta


def solution(mesh):
    placed = (
        P("alpha", "beta"),
        P(),
        P(),
        P(None, "beta"),
        P(None, "beta"),
        P(None, "beta"),
        P(None, "alpha"),
        P(None, "alpha"),
        P(None, "alpha"),
    )
    return jax.shard_map(
        shards, mesh=mesh, in_specs=placed, out_specs=P("alpha", "beta"), check_vma=False
    )
```

```python
import functools

import jax
import jax.numpy as jnp
from jax import lax
from jax.experimental import pallas as pl
from jax.experimental.pallas import tpu as pltpu
from jax.sharding import PartitionSpec as P

BF = jnp.bfloat16
F32 = jnp.float32
MESH = pl.DeviceIdType.MESH
NT = (((1,), (1,)), ((), ()))
TN = (((0,), (0,)), ((), ()))
LANES = 128
WIDE = 512
DS = 132
SS = 136
LS = 136
PICK_UNROLL = 4
DENS_UNROLL = 8


def iota(shape, dim):
    return lax.broadcasted_iota(jnp.int32, shape, dim)


def compute_kernel(
    hi_lane,
    ci_ref,
    one_ref,
    pair_ref,
    bt_ref,
    bp_ref,
    bs_ref,
    at_ref,
    ap_ref,
    as_ref,
    out_ref,
    rows_ref,
    part_ref,
    arrive_ref,
    one_pad_ref,
    pair_pad_ref,
    code_ref,
    turned_ref,
    group_ref,
    dens_ref,
    sv_ref,
    lift_ref,
    lift_bf_ref,
    wide_ref,
    picked_ref,
    beta_send,
    beta_recv,
    alpha_send,
    alpha_recv,
):
    blocks, rows, cols = rows_ref.shape
    excits = bt_ref.shape[0]
    slots = excits + 2
    per_group = LANES // slots
    groups = group_ref.shape[0]
    used_groups = -(-cols // per_group)
    me_beta = lax.axis_index("beta")
    me_alpha = lax.axis_index("alpha")
    strings = arrive_ref.shape[0]

    barrier = pltpu.get_barrier_semaphore()
    for r in range(1, blocks):
        peer = {"beta": lax.rem(me_beta + r, blocks)}
        pl.semaphore_signal(barrier, inc=1, device_id=peer, device_id_type=MESH)
    for r in range(1, strings):
        peer = {"alpha": lax.rem(me_alpha + r, strings)}
        pl.semaphore_signal(barrier, inc=1, device_id=peer, device_id_type=MESH)
    rows_ref[me_beta] = ci_ref[...].astype(BF)
    pl.semaphore_wait(barrier, blocks + strings - 2)

    def row_copy(source, target):
        return pltpu.make_async_remote_copy(
            src_ref=rows_ref.at[source],
            dst_ref=rows_ref.at[source],
            send_sem=beta_send.at[target],
            recv_sem=beta_recv.at[source],
            device_id={"beta": target},
            device_id_type=MESH,
        )

    def part_copy(source, target):
        return pltpu.make_async_remote_copy(
            src_ref=part_ref.at[target],
            dst_ref=arrive_ref.at[source],
            send_sem=alpha_send.at[target],
            recv_sem=alpha_recv.at[source],
            device_id={"alpha": target},
            device_id_type=MESH,
        )

    for r in range(1, blocks):
        row_copy(me_beta, lax.rem(me_beta + r, blocks)).start()

    code_ref[...] = jnp.zeros_like(code_ref)
    listed = bt_ref[...] + 2048 * bp_ref[...] + (1 << 18) * bs_ref[...]
    code_ref[0:excits, :] = listed.astype(F32)
    own = me_beta * cols + iota((8, cols), 1)
    extra = iota((8, cols), 0)
    own = jnp.where(extra < 2, own + 2048 * (hi_lane + extra) + (1 << 18), 0)
    code_ref[excits : excits + 8, :] = own.astype(F32)
    turned_ref[...] = jnp.zeros_like(turned_ref)
    turned_ref[0:cols, :] = code_ref[...].T
    grouped = turned_ref[pl.ds(0, groups, stride=per_group), :]
    for t in range(1, per_group):
        shifted = turned_ref[pl.ds(t, groups, stride=per_group), :]
        grouped = grouped + pltpu.roll(shifted, t * slots, 1)
    group_ref[...] = grouped.astype(jnp.int32)

    pairs = pair_ref.shape[0]
    one_pad_ref[...] = jnp.zeros_like(one_pad_ref)
    one_pad_ref[0:1, 0:pairs] = one_ref[...]
    pair_pad_ref[...] = jnp.zeros_like(pair_pad_ref)
    pair_pad_ref[0:pairs, 0:pairs] = pair_ref[...].astype(F32)
    one_row = one_pad_ref[0:1, :]
    one_hi = one_row.astype(BF).astype(F32)
    one_lo = one_row - one_hi
    one_two = jnp.concatenate([one_hi, one_lo, jnp.zeros((6, LANES), F32)], axis=0)
    one_cols = jnp.concatenate([one_two, jnp.zeros((LANES - 8, LANES), F32)], axis=0).T
    lane = iota((LANES, LANES), 1)
    table = pair_pad_ref[...]
    table = jnp.where(lane == hi_lane, one_cols[:, 0:1], table)
    table = jnp.where(lane == hi_lane + 1, one_cols[:, 1:2], table)
    table = table.astype(BF)

    def sv_step(e, carry):
        which = ap_ref[pl.ds(e, 1), :]
        sign = (2 * as_ref[pl.ds(e, 1), :] - 1).astype(F32)
        hot = jnp.where(iota((LANES, rows), 0) == which, sign, 0.0).astype(BF)
        sv = lax.dot_general(hot, table, TN, preferred_element_type=F32)
        sv_ref[pl.ds(pl.multiple_of(e * SS, 8), rows), :] = sv
        return carry

    lax.fori_loop(0, excits, sv_step, 0, unroll=8)
    for e, row in enumerate((one_hi, one_lo)):
        start = (excits + e) * SS
        sv_ref[start : start + rows, :] = jnp.broadcast_to(row, (rows, LANES))
    sv_ref[(excits + 2) * SS :, :] = jnp.zeros(((46 - excits) * SS, LANES), F32)

    for r in range(1, blocks):
        row_copy(lax.rem(me_beta + r, blocks), me_beta).wait_recv()

    wide = wide_ref.shape[1]
    parts = blocks * cols // wide
    joined = wide // cols
    for m in range(blocks):
        wide_ref[
            (m // joined) * rows : (m // joined + 1) * rows,
            (m % joined) * cols : (m % joined + 1) * cols,
        ] = rows_ref[m]
    lane_row = iota((1, LANES), 1)
    lane_slot = lane_row // slots

    def pick_step(step, carry):
        coded = [group_ref[pl.ds(2 * step + u, 1), :] for u in range(2)]
        code = jnp.concatenate(coded, axis=1)
        target = jnp.bitwise_and(code, 2047)
        low = jnp.bitwise_and(target, wide - 1)
        block = target // wide
        sign = (2 * lax.shift_right_logical(code, 18) - 1).astype(F32)
        pick = jnp.where(iota((wide, 2 * LANES), 0) == low, sign, 0.0).astype(BF)
        found = jnp.dot(wide_ref[...], pick, preferred_element_type=F32)
        picked = found[0:rows]
        for m in range(1, parts):
            picked = jnp.where(block == m, found[m * rows : (m + 1) * rows], picked)
        picked = picked.astype(BF)
        for u in range(2):
            picked_ref[2 * step + u] = picked[:, u * LANES : (u + 1) * LANES]
        return carry

    lax.fori_loop(0, used_groups // 2, pick_step, 0, unroll=PICK_UNROLL)

    def density_step(g, carry):
        code = group_ref[pl.ds(g, 1), :]
        pair = jnp.bitwise_and(lax.shift_right_logical(code, 11), 127)
        goal = jnp.where(lane_slot < per_group, lane_slot * LANES + pair, -1)
        spots = iota((per_group * LANES, LANES), 0) == goal
        hot = jnp.where(spots, 1.0, 0.0).astype(BF)
        dens = lax.dot_general(picked_ref[g], hot, NT, preferred_element_type=F32)
        for t in range(per_group):
            base = (per_group * g + t) * DS
            dens_ref[pl.ds(pl.multiple_of(base, 4), rows), :] = dens[
                :, t * LANES : (t + 1) * LANES
            ]
        return carry

    lax.fori_loop(0, used_groups, density_step, 0, unroll=DENS_UNROLL)

    def lift_step(a, carry):
        weights = sv_ref[pl.ds(a, 48, stride=SS), :].astype(BF)
        dens = dens_ref[pl.ds(a, cols, stride=DS), :].astype(BF)
        out = lax.dot_general(weights, dens, NT, preferred_element_type=F32)
        for half in range(2):
            lift_ref[half, pl.ds(a, 48, stride=LS), :] = out[:, half * LANES : (half + 1) * LANES]
        return carry

    lax.fori_loop(0, rows, lift_step, 0, unroll=16)
    for half in range(2):
        at_half = slice(half * LANES, (half + 1) * LANES)
        for e in range(excits):
            lift_bf_ref[e * rows : (e + 1) * rows, at_half] = lift_ref[
                half, e * LS : e * LS + rows, :
            ].astype(BF)

    tall = 4 * rows
    mine, place = me_alpha // 4, lax.rem(me_alpha, 4)
    turns = strings // 4

    def spread_step(s, carry):
        group = lax.rem(mine + 1 + s, turns)
        hots = []
        for e in range(excits):
            goal = at_ref[e : e + 1, :] - group * tall
            hots.append(jnp.where(iota((tall, rows), 0) == goal, 1.0, 0.0).astype(BF))
        hot = jnp.concatenate(hots, axis=1)
        out = jnp.dot(hot, lift_bf_ref[...], preferred_element_type=F32)
        for t in range(4):
            part_ref[4 * group + t] = out[t * rows : (t + 1) * rows].astype(BF)
        for t in range(4):
            target = 4 * group + lax.rem(place + 1 + t, 4)

            @pl.when(target != me_alpha)
            def _():
                part_copy(me_alpha, target).start()

        return carry

    lax.fori_loop(0, turns, spread_step, 0)

    for half in range(2):
        at_half = slice(half * LANES, (half + 1) * LANES)
        out_ref[:, at_half] = (
            lift_ref[half, excits * LS : excits * LS + rows, :]
            + lift_ref[half, (excits + 1) * LS : (excits + 1) * LS + rows, :]
        )
    total = out_ref[...] + part_ref[me_alpha].astype(F32)
    for r in range(1, strings):
        source = lax.rem(me_alpha + strings - r, strings)
        part_copy(source, me_alpha).wait_recv()
        total = total + arrive_ref[source].astype(F32)
    out_ref[...] = total
    for r in range(1, blocks):
        row_copy(me_beta, lax.rem(me_beta + r, blocks)).wait_send()
    for r in range(1, strings):
        part_copy(me_alpha, lax.rem(me_alpha + r, strings)).wait_send()


def shards(ci_vector, one_body, pair_integrals, bt, bp, bs, at, ap, asg):
    rows, cols = ci_vector.shape
    blocks, strings = lax.axis_size("beta"), lax.axis_size("alpha")
    pairs = one_body.shape[0]
    excits = bt.shape[0]
    per_group = LANES // (excits + 2)
    used = -(-cols // per_group)
    groups = -(-used // 8) * 8
    vmem = pl.BlockSpec(memory_space=pltpu.VMEM)
    return pl.pallas_call(
        functools.partial(compute_kernel, pairs),
        out_shape=jax.ShapeDtypeStruct((rows, cols), F32),
        in_specs=[vmem] * 9,
        out_specs=vmem,
        scratch_shapes=[
            pltpu.VMEM((blocks, rows, cols), BF),
            pltpu.VMEM((strings, rows, cols), BF),
            pltpu.VMEM((strings, rows, cols), BF),
            pltpu.VMEM((8, LANES), F32),
            pltpu.VMEM((LANES, LANES), F32),
            pltpu.VMEM((LANES, cols), F32),
            pltpu.VMEM((groups * per_group, LANES), F32),
            pltpu.VMEM((groups, LANES), jnp.int32),
            pltpu.VMEM((groups * per_group * DS, LANES), F32),
            pltpu.VMEM((48 * SS, LANES), F32),
            pltpu.VMEM((2, 48 * LS, LANES), F32),
            pltpu.VMEM((excits * rows, cols), BF),
            pltpu.VMEM((blocks * rows * cols // WIDE, WIDE), BF),
            pltpu.VMEM((groups, rows, LANES), BF),
            pltpu.SemaphoreType.DMA((blocks,)),
            pltpu.SemaphoreType.DMA((blocks,)),
            pltpu.SemaphoreType.DMA((strings,)),
            pltpu.SemaphoreType.DMA((strings,)),
        ],
        compiler_params=pltpu.CompilerParams(
            vmem_limit_bytes=56 * 2**20, collective_id=0, has_side_effects=True
        ),
    )(ci_vector, one_body.reshape(1, pairs), pair_integrals, bt, bp, bs, at, ap, asg)


def solution(mesh):
    placed = (
        P("alpha", "beta"),
        P(),
        P(),
        P(None, "beta"),
        P(None, "beta"),
        P(None, "beta"),
        P(None, "alpha"),
        P(None, "alpha"),
        P(None, "alpha"),
    )
    return jax.shard_map(
        shards, mesh=mesh, in_specs=placed, out_specs=P("alpha", "beta"), check_vma=False
    )
```

```python
import functools

import jax
import jax.numpy as jnp
from jax import lax
from jax.experimental import pallas as pl
from jax.experimental.pallas import tpu as pltpu
from jax.sharding import PartitionSpec as P

BF = jnp.bfloat16
F32 = jnp.float32
MESH = pl.DeviceIdType.MESH
NT = (((1,), (1,)), ((), ()))
TN = (((0,), (0,)), ((), ()))
LANES = 128
WIDE = 512
DS = 132
SS = 136
LS = 136
PICK_UNROLL = 4
DENS_UNROLL = 8


def iota(shape, dim):
    return lax.broadcasted_iota(jnp.int32, shape, dim)


def compute_kernel(
    hi_lane,
    ci_ref,
    one_ref,
    pair_ref,
    bt_ref,
    bp_ref,
    bs_ref,
    at_ref,
    ap_ref,
    as_ref,
    out_ref,
    rows_ref,
    near_part_ref,
    far_part_ref,
    near_got_ref,
    far_got_ref,
    last_part_ref,
    last_got_ref,
    one_pad_ref,
    pair_pad_ref,
    code_ref,
    turned_ref,
    group_ref,
    dens_ref,
    sv_ref,
    lift_ref,
    lift_bf_ref,
    wide_ref,
    picked_ref,
    order_ref,
    beta_send,
    beta_recv,
    near_send,
    near_recv,
    far_send,
    far_recv,
    last_send,
    last_recv,
):
    blocks, rows, cols = rows_ref.shape
    excits = bt_ref.shape[0]
    slots = excits + 2
    per_group = LANES // slots
    groups = group_ref.shape[0]
    used_groups = -(-cols // per_group)
    me_beta = lax.axis_index("beta")
    me_alpha = lax.axis_index("alpha")

    barrier = pltpu.get_barrier_semaphore()
    chips = blocks // 2
    here, core = me_beta // 2, lax.rem(me_beta, 2)
    sibling = 2 * here + 1 - core
    right = 2 * lax.rem(here + 1, chips) + core
    left = 2 * lax.rem(here + chips - 1, chips) + core
    across = 2 * lax.rem(here + 2, chips) + core
    beta_peers = (sibling, left, right, across)
    for peer in beta_peers:
        pl.semaphore_signal(barrier, inc=1, device_id={"beta": peer}, device_id_type=MESH)
    mine, place = me_alpha // 4, lax.rem(me_alpha, 4)

    def at_far(far):
        return {"alpha": 4 * far + place}

    def at_near(near):
        return {"alpha": 4 * mine + near}

    def turned(start, r):
        return lax.rem(start + r, 4)

    for r in range(1, 4):
        for peer in (at_far(turned(mine, r)), at_near(turned(place, r))):
            pl.semaphore_signal(barrier, inc=1, device_id=peer, device_id_type=MESH)
    rows_ref[me_beta] = ci_ref[...].astype(BF)
    pl.semaphore_wait(barrier, len(beta_peers) + 6)

    def row_copy(k, block, target):
        return pltpu.make_async_remote_copy(
            src_ref=rows_ref.at[block],
            dst_ref=rows_ref.at[block],
            send_sem=beta_send.at[k],
            recv_sem=beta_recv.at[k],
            device_id={"beta": target},
            device_id_type=MESH,
        )

    def other(block):
        return block + 1 - 2 * core

    sends = [
        row_copy(0, me_beta, across),
        row_copy(1, me_beta, right),
        row_copy(2, me_beta, left),
        row_copy(3, me_beta, sibling),
        row_copy(4, across, sibling),
        row_copy(5, left, sibling),
        row_copy(6, right, sibling),
    ]
    arrivals = [
        row_copy(0, across, me_beta),
        row_copy(1, left, me_beta),
        row_copy(2, right, me_beta),
        row_copy(3, sibling, me_beta),
        row_copy(4, other(across), me_beta),
        row_copy(5, other(left), me_beta),
        row_copy(6, other(right), me_beta),
    ]

    def near_copy(source, target):
        return pltpu.make_async_remote_copy(
            src_ref=near_part_ref.at[target],
            dst_ref=near_got_ref.at[source],
            send_sem=near_send.at[target],
            recv_sem=near_recv.at[source],
            device_id=at_near(target),
            device_id_type=MESH,
        )

    def far_copy(source, target, near):
        return pltpu.make_async_remote_copy(
            src_ref=far_part_ref.at[near, target],
            dst_ref=far_got_ref.at[source, near],
            send_sem=far_send.at[near, target],
            recv_sem=far_recv.at[source, near],
            device_id=at_far(target),
            device_id_type=MESH,
        )

    def near_last(source, target):
        return pltpu.make_async_remote_copy(
            src_ref=last_part_ref.at[1, target],
            dst_ref=last_got_ref.at[1, source],
            send_sem=last_send.at[1, target],
            recv_sem=last_recv.at[1, source],
            device_id=at_near(target),
            device_id_type=MESH,
        )

    def far_last(source, target):
        return pltpu.make_async_remote_copy(
            src_ref=last_part_ref.at[0, target],
            dst_ref=last_got_ref.at[0, source],
            send_sem=last_send.at[0, target],
            recv_sem=last_recv.at[0, source],
            device_id=at_far(target),
            device_id_type=MESH,
        )

    for k in range(4):
        sends[k].start()

    code_ref[...] = jnp.zeros_like(code_ref)
    listed = bt_ref[...] + 2048 * bp_ref[...] + (1 << 18) * bs_ref[...]
    code_ref[0:excits, :] = listed.astype(F32)
    own = me_beta * cols + iota((8, cols), 1)
    extra = iota((8, cols), 0)
    own = jnp.where(extra < 2, own + 2048 * (hi_lane + extra) + (1 << 18), 0)
    code_ref[excits : excits + 8, :] = own.astype(F32)
    turned_ref[...] = jnp.zeros_like(turned_ref)
    turned_ref[0:cols, :] = code_ref[...].T
    grouped = turned_ref[pl.ds(0, groups, stride=per_group), :]
    for t in range(1, per_group):
        shifted = turned_ref[pl.ds(t, groups, stride=per_group), :]
        grouped = grouped + pltpu.roll(shifted, t * slots, 1)
    group_ref[...] = grouped.astype(jnp.int32)

    device = at_ref[...] // rows
    near = jnp.bitwise_and(jnp.bitwise_and(device, 3) - place + 3, 3)
    order_ref[...] = (4 * near + device // 4) * rows + jnp.bitwise_and(at_ref[...], rows - 1)

    pairs = pair_ref.shape[0]
    one_pad_ref[...] = jnp.zeros_like(one_pad_ref)
    one_pad_ref[0:1, 0:pairs] = one_ref[...]
    pair_pad_ref[...] = jnp.zeros_like(pair_pad_ref)
    pair_pad_ref[0:pairs, 0:pairs] = pair_ref[...].astype(F32)
    one_row = one_pad_ref[0:1, :]
    one_hi = one_row.astype(BF).astype(F32)
    one_lo = one_row - one_hi
    one_two = jnp.concatenate([one_hi, one_lo, jnp.zeros((6, LANES), F32)], axis=0)
    one_cols = jnp.concatenate([one_two, jnp.zeros((LANES - 8, LANES), F32)], axis=0).T
    lane = iota((LANES, LANES), 1)
    table = pair_pad_ref[...]
    table = jnp.where(lane == hi_lane, one_cols[:, 0:1], table)
    table = jnp.where(lane == hi_lane + 1, one_cols[:, 1:2], table)
    table = table.astype(BF)

    def sv_step(e, carry):
        which = ap_ref[pl.ds(e, 1), :]
        sign = (2 * as_ref[pl.ds(e, 1), :] - 1).astype(F32)
        hot = jnp.where(iota((LANES, rows), 0) == which, sign, 0.0).astype(BF)
        sv = lax.dot_general(hot, table, TN, preferred_element_type=F32)
        sv_ref[pl.ds(pl.multiple_of(e * SS, 8), rows), :] = sv
        return carry

    lax.fori_loop(0, excits, sv_step, 0, unroll=8)
    for e, row in enumerate((one_hi, one_lo)):
        start = (excits + e) * SS
        sv_ref[start : start + rows, :] = jnp.broadcast_to(row, (rows, LANES))
    sv_ref[(excits + 2) * SS :, :] = jnp.zeros(((46 - excits) * SS, LANES), F32)

    for k, passed in ((1, 5), (2, 6), (0, 4)):
        arrivals[k].wait_recv()
        sends[passed].start()
    for k in (3, 5, 6, 4):
        arrivals[k].wait_recv()

    wide = wide_ref.shape[1]
    parts = blocks * cols // wide
    joined = wide // cols
    for m in range(blocks):
        wide_ref[
            (m // joined) * rows : (m // joined + 1) * rows,
            (m % joined) * cols : (m % joined + 1) * cols,
        ] = rows_ref[m]
    lane_row = iota((1, LANES), 1)
    lane_slot = lane_row // slots

    def pick_step(step, carry):
        coded = [group_ref[pl.ds(2 * step + u, 1), :] for u in range(2)]
        code = jnp.concatenate(coded, axis=1)
        target = jnp.bitwise_and(code, 2047)
        low = jnp.bitwise_and(target, wide - 1)
        block = target // wide
        sign = (2 * lax.shift_right_logical(code, 18) - 1).astype(F32)
        pick = jnp.where(iota((wide, 2 * LANES), 0) == low, sign, 0.0).astype(BF)
        found = jnp.dot(wide_ref[...], pick, preferred_element_type=F32)
        picked = found[0:rows]
        for m in range(1, parts):
            picked = jnp.where(block == m, found[m * rows : (m + 1) * rows], picked)
        picked = picked.astype(BF)
        for u in range(2):
            picked_ref[2 * step + u] = picked[:, u * LANES : (u + 1) * LANES]
        return carry

    lax.fori_loop(0, used_groups // 2, pick_step, 0, unroll=PICK_UNROLL)

    def density_step(g, carry):
        code = group_ref[pl.ds(g, 1), :]
        pair = jnp.bitwise_and(lax.shift_right_logical(code, 11), 127)
        goal = jnp.where(lane_slot < per_group, lane_slot * LANES + pair, -1)
        spots = iota((per_group * LANES, LANES), 0) == goal
        hot = jnp.where(spots, 1.0, 0.0).astype(BF)
        dens = lax.dot_general(picked_ref[g], hot, NT, preferred_element_type=F32)
        for t in range(per_group):
            base = (per_group * g + t) * DS
            dens_ref[pl.ds(pl.multiple_of(base, 4), rows), :] = dens[
                :, t * LANES : (t + 1) * LANES
            ]
        return carry

    lax.fori_loop(0, used_groups, density_step, 0, unroll=DENS_UNROLL)

    def lift_step(a, carry):
        weights = sv_ref[pl.ds(a, 48, stride=SS), :].astype(BF)
        dens = dens_ref[pl.ds(a, cols, stride=DS), :].astype(BF)
        out = lax.dot_general(weights, dens, NT, preferred_element_type=F32)
        for half in range(2):
            lift_ref[half, pl.ds(a, 48, stride=LS), :] = out[:, half * LANES : (half + 1) * LANES]
        return carry

    lax.fori_loop(0, rows, lift_step, 0, unroll=16)
    for half in range(2):
        at_half = slice(half * LANES, (half + 1) * LANES)
        for e in range(excits):
            lift_bf_ref[e * rows : (e + 1) * rows, at_half] = lift_ref[
                half, e * LS : e * LS + rows, :
            ].astype(BF)

    tall = 4 * rows

    def spread_step(s, carry):
        hots = []
        for e in range(excits):
            goal = order_ref[e : e + 1, :] - s * tall
            hots.append(jnp.where(iota((tall, rows), 0) == goal, 1.0, 0.0).astype(BF))
        hot = jnp.concatenate(hots, axis=1)
        out = jnp.dot(hot, lift_bf_ref[...], preferred_element_type=F32).astype(BF)
        near = turned(place, s + 1)
        for far in range(4):
            at_rows = slice(far * rows, (far + 1) * rows)
            near_part_ref[near, far] = out[at_rows, 0:LANES]
            far_part_ref[near, far] = out[at_rows, LANES : 2 * LANES]

        @pl.when(s < 3)
        def _():
            near_copy(place, near).start()

        for r in (2, 1, 3):
            far_copy(mine, turned(mine, r), near).start()
        return carry

    lax.fori_loop(0, 4, spread_step, 0)

    for half in range(2):
        at_half = slice(half * LANES, (half + 1) * LANES)
        out_ref[:, at_half] = (
            lift_ref[half, excits * LS : excits * LS + rows, :]
            + lift_ref[half, (excits + 1) * LS : (excits + 1) * LS + rows, :]
        )

    for r in range(1, 4):
        near_copy(turned(place, r), place).wait_recv()
    for r in (2, 1, 3, 0):
        far = turned(mine, r)
        total = near_part_ref[place, far].astype(F32)
        for q in range(1, 4):
            total = total + near_got_ref[turned(place, q), far].astype(F32)
        if r:
            last_part_ref[0, far] = total.astype(BF)
            far_last(mine, far).start()
        else:
            out_ref[:, 0:LANES] = out_ref[:, 0:LANES] + total

    for r in (2, 1, 3, 0):
        near = turned(place, r)
        total = far_part_ref[near, mine].astype(F32)
        for q in range(1, 4):
            source = turned(mine, q)
            far_copy(source, mine, near).wait_recv()
            total = total + far_got_ref[source, near].astype(F32)
        if r:
            last_part_ref[1, near] = total.astype(BF)
            near_last(place, near).start()
        else:
            out_ref[:, LANES : 2 * LANES] = out_ref[:, LANES : 2 * LANES] + total

    total = out_ref[:, 0:LANES]
    for r in range(1, 4):
        far_last(turned(mine, r), mine).wait_recv()
        total = total + last_got_ref[0, turned(mine, r)].astype(F32)
    out_ref[:, 0:LANES] = total
    total = out_ref[:, LANES : 2 * LANES]
    for r in range(1, 4):
        near_last(turned(place, r), place).wait_recv()
        total = total + last_got_ref[1, turned(place, r)].astype(F32)
    out_ref[:, LANES : 2 * LANES] = total

    for copy in sends:
        copy.wait_send()
    for r in range(1, 4):
        near_copy(place, turned(place, r)).wait_send()
        far_last(mine, turned(mine, r)).wait_send()
        near_last(place, turned(place, r)).wait_send()
        for near in range(4):
            far_copy(mine, turned(mine, r), near).wait_send()


def shards(ci_vector, one_body, pair_integrals, bt, bp, bs, at, ap, asg):
    rows, cols = ci_vector.shape
    blocks = lax.axis_size("beta")
    pairs = one_body.shape[0]
    excits = bt.shape[0]
    per_group = LANES // (excits + 2)
    used = -(-cols // per_group)
    groups = -(-used // 8) * 8
    vmem = pl.BlockSpec(memory_space=pltpu.VMEM)
    return pl.pallas_call(
        functools.partial(compute_kernel, pairs),
        out_shape=jax.ShapeDtypeStruct((rows, cols), F32),
        in_specs=[vmem] * 9,
        out_specs=vmem,
        scratch_shapes=[
            pltpu.VMEM((blocks, rows, cols), BF),
            pltpu.VMEM((4, 4, rows, LANES), BF),
            pltpu.VMEM((4, 4, rows, LANES), BF),
            pltpu.VMEM((4, 4, rows, LANES), BF),
            pltpu.VMEM((4, 4, rows, LANES), BF),
            pltpu.VMEM((2, 4, rows, LANES), BF),
            pltpu.VMEM((2, 4, rows, LANES), BF),
            pltpu.VMEM((8, LANES), F32),
            pltpu.VMEM((LANES, LANES), F32),
            pltpu.VMEM((LANES, cols), F32),
            pltpu.VMEM((groups * per_group, LANES), F32),
            pltpu.VMEM((groups, LANES), jnp.int32),
            pltpu.VMEM((groups * per_group * DS, LANES), F32),
            pltpu.VMEM((48 * SS, LANES), F32),
            pltpu.VMEM((2, 48 * LS, LANES), F32),
            pltpu.VMEM((excits * rows, cols), BF),
            pltpu.VMEM((blocks * rows * cols // WIDE, WIDE), BF),
            pltpu.VMEM((groups, rows, LANES), BF),
            pltpu.VMEM((excits, rows), jnp.int32),
            pltpu.SemaphoreType.DMA((blocks,)),
            pltpu.SemaphoreType.DMA((blocks,)),
            pltpu.SemaphoreType.DMA((4,)),
            pltpu.SemaphoreType.DMA((4,)),
            pltpu.SemaphoreType.DMA((4, 4)),
            pltpu.SemaphoreType.DMA((4, 4)),
            pltpu.SemaphoreType.DMA((2, 4)),
            pltpu.SemaphoreType.DMA((2, 4)),
        ],
        compiler_params=pltpu.CompilerParams(
            vmem_limit_bytes=56 * 2**20, collective_id=0, has_side_effects=True
        ),
    )(ci_vector, one_body.reshape(1, pairs), pair_integrals, bt, bp, bs, at, ap, asg)


def solution(mesh):
    placed = (
        P("alpha", "beta"),
        P(),
        P(),
        P(None, "beta"),
        P(None, "beta"),
        P(None, "beta"),
        P(None, "alpha"),
        P(None, "alpha"),
        P(None, "alpha"),
    )
    return jax.shard_map(
        shards, mesh=mesh, in_specs=placed, out_specs=P("alpha", "beta"), check_vma=False
    )
```

```python
import functools

import jax
import jax.numpy as jnp
from jax import lax
from jax.experimental import pallas as pl
from jax.experimental.pallas import tpu as pltpu
from jax.sharding import PartitionSpec as P

BF = jnp.bfloat16
F32 = jnp.float32
MESH = pl.DeviceIdType.MESH
NT = (((1,), (1,)), ((), ()))
TN = (((0,), (0,)), ((), ()))
LANES = 128
WIDE = 512
DS = 132
SS = 136
LS = 136
BATCH = 4


def iota(shape, dim):
    return lax.broadcasted_iota(jnp.int32, shape, dim)


def compute_kernel(
    hi_lane,
    ci_ref,
    one_ref,
    pair_ref,
    bt_ref,
    bp_ref,
    bs_ref,
    at_ref,
    ap_ref,
    as_ref,
    out_ref,
    rows_ref,
    near_part_ref,
    far_part_ref,
    near_got_ref,
    far_got_ref,
    last_part_ref,
    last_got_ref,
    one_pad_ref,
    pair_pad_ref,
    code_ref,
    turned_ref,
    group_ref,
    dens_ref,
    sv_ref,
    lift_ref,
    lift_bf_ref,
    wide_ref,
    even_ref,
    odd_ref,
    order_ref,
    beta_send,
    beta_recv,
    near_send,
    near_recv,
    far_send,
    far_recv,
    last_send,
    last_recv,
):
    blocks, rows, cols = rows_ref.shape
    excits = bt_ref.shape[0]
    slots = excits + 2
    per_group = LANES // slots
    groups = group_ref.shape[0]
    me_beta = lax.axis_index("beta")
    me_alpha = lax.axis_index("alpha")

    barrier = pltpu.get_barrier_semaphore()
    chips = blocks // 2
    here, core = me_beta // 2, lax.rem(me_beta, 2)
    sibling = 2 * here + 1 - core
    right = 2 * lax.rem(here + 1, chips) + core
    left = 2 * lax.rem(here + chips - 1, chips) + core
    across = 2 * lax.rem(here + 2, chips) + core
    beta_peers = (sibling, left, right, across)
    for peer in beta_peers:
        pl.semaphore_signal(barrier, inc=1, device_id={"beta": peer}, device_id_type=MESH)
    mine, place = me_alpha // 4, lax.rem(me_alpha, 4)

    def at_far(far):
        return {"alpha": 4 * far + place}

    def at_near(near):
        return {"alpha": 4 * mine + near}

    def turned(start, r):
        return lax.rem(start + r, 4)

    for r in range(1, 4):
        for peer in (at_far(turned(mine, r)), at_near(turned(place, r))):
            pl.semaphore_signal(barrier, inc=1, device_id=peer, device_id_type=MESH)
    rows_ref[me_beta] = ci_ref[...].astype(BF)
    pl.semaphore_wait(barrier, len(beta_peers) + 6)

    def row_copy(k, block, target):
        return pltpu.make_async_remote_copy(
            src_ref=rows_ref.at[block],
            dst_ref=rows_ref.at[block],
            send_sem=beta_send.at[k],
            recv_sem=beta_recv.at[k],
            device_id={"beta": target},
            device_id_type=MESH,
        )

    def other(block):
        return block + 1 - 2 * core

    sends = [
        row_copy(0, me_beta, across),
        row_copy(1, me_beta, right),
        row_copy(2, me_beta, left),
        row_copy(3, me_beta, sibling),
        row_copy(4, across, sibling),
        row_copy(5, left, sibling),
        row_copy(6, right, sibling),
    ]
    arrivals = [
        row_copy(0, across, me_beta),
        row_copy(1, left, me_beta),
        row_copy(2, right, me_beta),
        row_copy(3, sibling, me_beta),
        row_copy(4, other(across), me_beta),
        row_copy(5, other(left), me_beta),
        row_copy(6, other(right), me_beta),
    ]

    def near_copy(source, target):
        return pltpu.make_async_remote_copy(
            src_ref=near_part_ref.at[target],
            dst_ref=near_got_ref.at[source],
            send_sem=near_send.at[target],
            recv_sem=near_recv.at[source],
            device_id=at_near(target),
            device_id_type=MESH,
        )

    def far_copy(source, target, near):
        return pltpu.make_async_remote_copy(
            src_ref=far_part_ref.at[near, target],
            dst_ref=far_got_ref.at[source, near],
            send_sem=far_send.at[near, target],
            recv_sem=far_recv.at[source, near],
            device_id=at_far(target),
            device_id_type=MESH,
        )

    def near_last(source, target):
        return pltpu.make_async_remote_copy(
            src_ref=last_part_ref.at[1, target],
            dst_ref=last_got_ref.at[1, source],
            send_sem=last_send.at[1, target],
            recv_sem=last_recv.at[1, source],
            device_id=at_near(target),
            device_id_type=MESH,
        )

    def far_last(source, target):
        return pltpu.make_async_remote_copy(
            src_ref=last_part_ref.at[0, target],
            dst_ref=last_got_ref.at[0, source],
            send_sem=last_send.at[0, target],
            recv_sem=last_recv.at[0, source],
            device_id=at_far(target),
            device_id_type=MESH,
        )

    for k in range(4):
        sends[k].start()

    code_ref[...] = jnp.zeros_like(code_ref)
    listed = bt_ref[...] + 2048 * bp_ref[...] + (1 << 18) * bs_ref[...]
    code_ref[0:excits, :] = listed.astype(F32)
    own = me_beta * cols + iota((8, cols), 1)
    extra = iota((8, cols), 0)
    own = jnp.where(extra < 2, own + 2048 * (hi_lane + extra) + (1 << 18), 0)
    code_ref[excits : excits + 8, :] = own.astype(F32)
    turned_ref[...] = jnp.zeros_like(turned_ref)
    turned_ref[0:cols, :] = code_ref[...].T
    grouped = turned_ref[pl.ds(0, groups, stride=per_group), :]
    for t in range(1, per_group):
        shifted = turned_ref[pl.ds(t, groups, stride=per_group), :]
        grouped = grouped + pltpu.roll(shifted, t * slots, 1)
    group_ref[...] = grouped.astype(jnp.int32)

    device = at_ref[...] // rows
    near = jnp.bitwise_and(jnp.bitwise_and(device, 3) - place + 3, 3)
    order_ref[...] = (4 * near + device // 4) * rows + jnp.bitwise_and(at_ref[...], rows - 1)

    pairs = pair_ref.shape[0]
    one_pad_ref[...] = jnp.zeros_like(one_pad_ref)
    one_pad_ref[0:1, 0:pairs] = one_ref[...]
    pair_pad_ref[...] = jnp.zeros_like(pair_pad_ref)
    pair_pad_ref[0:pairs, 0:pairs] = pair_ref[...].astype(F32)
    one_row = one_pad_ref[0:1, :]
    one_hi = one_row.astype(BF).astype(F32)
    one_lo = one_row - one_hi
    one_two = jnp.concatenate([one_hi, one_lo, jnp.zeros((6, LANES), F32)], axis=0)
    one_cols = jnp.concatenate([one_two, jnp.zeros((LANES - 8, LANES), F32)], axis=0).T
    lane = iota((LANES, LANES), 1)
    table = pair_pad_ref[...]
    table = jnp.where(lane == hi_lane, one_cols[:, 0:1], table)
    table = jnp.where(lane == hi_lane + 1, one_cols[:, 1:2], table)
    table = table.astype(BF)

    def sv_step(e, carry):
        which = ap_ref[pl.ds(e, 1), :]
        sign = (2 * as_ref[pl.ds(e, 1), :] - 1).astype(F32)
        hot = jnp.where(iota((LANES, rows), 0) == which, sign, 0.0).astype(BF)
        sv = lax.dot_general(hot, table, TN, preferred_element_type=F32)
        sv_ref[pl.ds(pl.multiple_of(e * SS, 8), rows), :] = sv
        return carry

    lax.fori_loop(0, excits, sv_step, 0, unroll=8)
    for e, row in enumerate((one_hi, one_lo)):
        start = (excits + e) * SS
        sv_ref[start : start + rows, :] = jnp.broadcast_to(row, (rows, LANES))
    sv_ref[(excits + 2) * SS :, :] = jnp.zeros(((46 - excits) * SS, LANES), F32)

    for k, passed in ((1, 5), (2, 6), (0, 4)):
        arrivals[k].wait_recv()
        sends[passed].start()
    for k in (3, 5, 6, 4):
        arrivals[k].wait_recv()

    wide = wide_ref.shape[1]
    parts = blocks * cols // wide
    joined = wide // cols
    for m in range(blocks):
        wide_ref[
            (m // joined) * rows : (m // joined + 1) * rows,
            (m % joined) * cols : (m % joined + 1) * cols,
        ] = rows_ref[m]
    lane_row = iota((1, LANES), 1)
    lane_slot = lane_row // slots

    def pick_step(step, held, slot):
        coded = [group_ref[pl.ds(2 * step + u, 1), :] for u in range(2)]
        code = jnp.concatenate(coded, axis=1)
        target = jnp.bitwise_and(code, 2047)
        low = jnp.bitwise_and(target, wide - 1)
        block = target // wide
        sign = (2 * lax.shift_right_logical(code, 18) - 1).astype(F32)
        pick = jnp.where(iota((wide, 2 * LANES), 0) == low, sign, 0.0).astype(BF)
        found = jnp.dot(wide_ref[...], pick, preferred_element_type=F32)
        picked = found[0:rows]
        for m in range(1, parts):
            picked = jnp.where(block == m, found[m * rows : (m + 1) * rows], picked)
        picked = picked.astype(BF)
        for u in range(2):
            held[2 * slot + u] = picked[:, u * LANES : (u + 1) * LANES]


    def density_step(g, held, slot):
        code = group_ref[pl.ds(g, 1), :]
        pair = jnp.bitwise_and(lax.shift_right_logical(code, 11), 127)
        goal = jnp.where(lane_slot < per_group, lane_slot * LANES + pair, -1)
        spots = iota((per_group * LANES, LANES), 0) == goal
        hot = jnp.where(spots, 1.0, 0.0).astype(BF)
        dens = lax.dot_general(held[slot], hot, NT, preferred_element_type=F32)
        for t in range(per_group):
            base = (per_group * g + t) * DS
            dens_ref[pl.ds(pl.multiple_of(base, 4), rows), :] = dens[
                :, t * LANES : (t + 1) * LANES
            ]

    def both(j, last, held):
        for u in range(BATCH):
            if held is not None:
                pick_step(BATCH * j + u, held, u)
            if last is not None:
                for v in (2 * u, 2 * u + 1):
                    density_step(2 * BATCH * (j - 1) + v, last, v)

    def both_step(k, carry):
        both(2 * k + 1, even_ref, odd_ref)
        both(2 * k + 2, odd_ref, even_ref)
        return carry

    batches = groups // (2 * BATCH)
    both(0, None, even_ref)
    lax.fori_loop(0, (batches - 1) // 2, both_step, 0)
    if batches % 2:
        both(batches, even_ref, None)
    else:
        both(batches - 1, even_ref, odd_ref)
        both(batches, odd_ref, None)

    def lift_step(a, carry):
        weights = sv_ref[pl.ds(a, 48, stride=SS), :].astype(BF)
        dens = dens_ref[pl.ds(a, cols, stride=DS), :].astype(BF)
        out = lax.dot_general(weights, dens, NT, preferred_element_type=F32)
        for half in range(2):
            lift_ref[half, pl.ds(a, 48, stride=LS), :] = out[:, half * LANES : (half + 1) * LANES]
        return carry

    lax.fori_loop(0, rows, lift_step, 0, unroll=16)
    for half in range(2):
        at_half = slice(half * LANES, (half + 1) * LANES)
        for e in range(excits):
            lift_bf_ref[e * rows : (e + 1) * rows, at_half] = lift_ref[
                half, e * LS : e * LS + rows, :
            ].astype(BF)

    tall = 4 * rows

    def spread_step(s, carry):
        hots = []
        for e in range(excits):
            goal = order_ref[e : e + 1, :] - s * tall
            hots.append(jnp.where(iota((tall, rows), 0) == goal, 1.0, 0.0).astype(BF))
        hot = jnp.concatenate(hots, axis=1)
        out = jnp.dot(hot, lift_bf_ref[...], preferred_element_type=F32).astype(BF)
        near = turned(place, s + 1)
        for far in range(4):
            at_rows = slice(far * rows, (far + 1) * rows)
            near_part_ref[near, far] = out[at_rows, 0:LANES]
            far_part_ref[near, far] = out[at_rows, LANES : 2 * LANES]

        @pl.when(s < 3)
        def _():
            near_copy(place, near).start()

        for r in (2, 1, 3):
            far_copy(mine, turned(mine, r), near).start()
        return carry

    lax.fori_loop(0, 4, spread_step, 0)

    for half in range(2):
        at_half = slice(half * LANES, (half + 1) * LANES)
        out_ref[:, at_half] = (
            lift_ref[half, excits * LS : excits * LS + rows, :]
            + lift_ref[half, (excits + 1) * LS : (excits + 1) * LS + rows, :]
        )

    for r in range(1, 4):
        near_copy(turned(place, r), place).wait_recv()
    for r in (2, 1, 3, 0):
        far = turned(mine, r)
        total = near_part_ref[place, far].astype(F32)
        for q in range(1, 4):
            total = total + near_got_ref[turned(place, q), far].astype(F32)
        if r:
            last_part_ref[0, far] = total.astype(BF)
            far_last(mine, far).start()
        else:
            out_ref[:, 0:LANES] = out_ref[:, 0:LANES] + total

    for r in (2, 1, 3, 0):
        near = turned(place, r)
        total = far_part_ref[near, mine].astype(F32)
        for q in range(1, 4):
            source = turned(mine, q)
            far_copy(source, mine, near).wait_recv()
            total = total + far_got_ref[source, near].astype(F32)
        if r:
            last_part_ref[1, near] = total.astype(BF)
            near_last(place, near).start()
        else:
            out_ref[:, LANES : 2 * LANES] = out_ref[:, LANES : 2 * LANES] + total

    total = out_ref[:, 0:LANES]
    for r in range(1, 4):
        far_last(turned(mine, r), mine).wait_recv()
        total = total + last_got_ref[0, turned(mine, r)].astype(F32)
    out_ref[:, 0:LANES] = total
    total = out_ref[:, LANES : 2 * LANES]
    for r in range(1, 4):
        near_last(turned(place, r), place).wait_recv()
        total = total + last_got_ref[1, turned(place, r)].astype(F32)
    out_ref[:, LANES : 2 * LANES] = total

    for copy in sends:
        copy.wait_send()
    for r in range(1, 4):
        near_copy(place, turned(place, r)).wait_send()
        far_last(mine, turned(mine, r)).wait_send()
        near_last(place, turned(place, r)).wait_send()
        for near in range(4):
            far_copy(mine, turned(mine, r), near).wait_send()


def shards(ci_vector, one_body, pair_integrals, bt, bp, bs, at, ap, asg):
    rows, cols = ci_vector.shape
    blocks = lax.axis_size("beta")
    pairs = one_body.shape[0]
    excits = bt.shape[0]
    per_group = LANES // (excits + 2)
    used = -(-cols // per_group)
    groups = -(-used // (2 * BATCH)) * 2 * BATCH
    vmem = pl.BlockSpec(memory_space=pltpu.VMEM)
    return pl.pallas_call(
        functools.partial(compute_kernel, pairs),
        out_shape=jax.ShapeDtypeStruct((rows, cols), F32),
        in_specs=[vmem] * 9,
        out_specs=vmem,
        scratch_shapes=[
            pltpu.VMEM((blocks, rows, cols), BF),
            pltpu.VMEM((4, 4, rows, LANES), BF),
            pltpu.VMEM((4, 4, rows, LANES), BF),
            pltpu.VMEM((4, 4, rows, LANES), BF),
            pltpu.VMEM((4, 4, rows, LANES), BF),
            pltpu.VMEM((2, 4, rows, LANES), BF),
            pltpu.VMEM((2, 4, rows, LANES), BF),
            pltpu.VMEM((8, LANES), F32),
            pltpu.VMEM((LANES, LANES), F32),
            pltpu.VMEM((LANES, cols), F32),
            pltpu.VMEM((groups * per_group, LANES), F32),
            pltpu.VMEM((groups, LANES), jnp.int32),
            pltpu.VMEM((groups * per_group * DS, LANES), F32),
            pltpu.VMEM((48 * SS, LANES), F32),
            pltpu.VMEM((2, 48 * LS, LANES), F32),
            pltpu.VMEM((excits * rows, cols), BF),
            pltpu.VMEM((blocks * rows * cols // WIDE, WIDE), BF),
            pltpu.VMEM((2 * BATCH, rows, LANES), BF),
            pltpu.VMEM((2 * BATCH, rows, LANES), BF),
            pltpu.VMEM((excits, rows), jnp.int32),
            pltpu.SemaphoreType.DMA((blocks,)),
            pltpu.SemaphoreType.DMA((blocks,)),
            pltpu.SemaphoreType.DMA((4,)),
            pltpu.SemaphoreType.DMA((4,)),
            pltpu.SemaphoreType.DMA((4, 4)),
            pltpu.SemaphoreType.DMA((4, 4)),
            pltpu.SemaphoreType.DMA((2, 4)),
            pltpu.SemaphoreType.DMA((2, 4)),
        ],
        compiler_params=pltpu.CompilerParams(
            vmem_limit_bytes=56 * 2**20, collective_id=0, has_side_effects=True
        ),
    )(ci_vector, one_body.reshape(1, pairs), pair_integrals, bt, bp, bs, at, ap, asg)


def solution(mesh):
    placed = (
        P("alpha", "beta"),
        P(),
        P(),
        P(None, "beta"),
        P(None, "beta"),
        P(None, "beta"),
        P(None, "alpha"),
        P(None, "alpha"),
        P(None, "alpha"),
    )
    return jax.shard_map(
        shards, mesh=mesh, in_specs=placed, out_specs=P("alpha", "beta"), check_vma=False
    )
```

```python
import functools

import jax
import jax.numpy as jnp
from jax import lax
from jax.experimental import pallas as pl
from jax.experimental.pallas import tpu as pltpu
from jax.sharding import PartitionSpec as P

BF = jnp.bfloat16
F32 = jnp.float32
MESH = pl.DeviceIdType.MESH
NT = (((1,), (1,)), ((), ()))
TN = (((0,), (0,)), ((), ()))
LANES = 128
WIDE = 512
DS = 132
SS = 136
LS = 136
BATCH = 4


def iota(shape, dim):
    return lax.broadcasted_iota(jnp.int32, shape, dim)


def compute_kernel(
    hi_lane,
    ci_ref,
    one_ref,
    pair_ref,
    bt_ref,
    bp_ref,
    bs_ref,
    at_ref,
    ap_ref,
    as_ref,
    out_ref,
    rows_ref,
    near_part_ref,
    far_part_ref,
    near_got_ref,
    far_got_ref,
    last_part_ref,
    last_got_ref,
    one_pad_ref,
    pair_pad_ref,
    code_ref,
    turned_ref,
    group_ref,
    dens_ref,
    sv_ref,
    lift_ref,
    lift_bf_ref,
    wide_ref,
    own_ref,
    even_ref,
    odd_ref,
    order_ref,
    beta_send,
    beta_recv,
    near_send,
    near_recv,
    far_send,
    far_recv,
    last_send,
    last_recv,
):
    blocks, rows, cols = rows_ref.shape
    excits = bt_ref.shape[0]
    slots = excits + 2
    per_group = LANES // slots
    groups = group_ref.shape[0]
    me_beta = lax.axis_index("beta")
    me_alpha = lax.axis_index("alpha")

    barrier = pltpu.get_barrier_semaphore()
    chips = blocks // 2
    here, core = me_beta // 2, lax.rem(me_beta, 2)
    sibling = 2 * here + 1 - core
    right = 2 * lax.rem(here + 1, chips) + core
    left = 2 * lax.rem(here + chips - 1, chips) + core
    across = 2 * lax.rem(here + 2, chips) + core
    beta_peers = (sibling, left, right, across)
    for peer in beta_peers:
        pl.semaphore_signal(barrier, inc=1, device_id={"beta": peer}, device_id_type=MESH)
    mine, place = me_alpha // 4, lax.rem(me_alpha, 4)

    def at_far(far):
        return {"alpha": 4 * far + place}

    def at_near(near):
        return {"alpha": 4 * mine + near}

    def turned(start, r):
        return lax.rem(start + r, 4)

    for r in range(1, 4):
        for peer in (at_far(turned(mine, r)), at_near(turned(place, r))):
            pl.semaphore_signal(barrier, inc=1, device_id=peer, device_id_type=MESH)
    rows_ref[me_beta] = ci_ref[...].astype(BF)
    pl.semaphore_wait(barrier, len(beta_peers) + 6)

    def row_copy(k, block, target):
        return pltpu.make_async_remote_copy(
            src_ref=rows_ref.at[block],
            dst_ref=rows_ref.at[block],
            send_sem=beta_send.at[k],
            recv_sem=beta_recv.at[k],
            device_id={"beta": target},
            device_id_type=MESH,
        )

    def other(block):
        return block + 1 - 2 * core

    sends = [
        row_copy(0, me_beta, across),
        row_copy(1, me_beta, right),
        row_copy(2, me_beta, left),
        row_copy(3, me_beta, sibling),
        row_copy(4, across, sibling),
        row_copy(5, left, sibling),
        row_copy(6, right, sibling),
    ]
    arrivals = [
        row_copy(0, across, me_beta),
        row_copy(1, left, me_beta),
        row_copy(2, right, me_beta),
        row_copy(3, sibling, me_beta),
        row_copy(4, other(across), me_beta),
        row_copy(5, other(left), me_beta),
        row_copy(6, other(right), me_beta),
    ]

    def near_copy(source, target):
        return pltpu.make_async_remote_copy(
            src_ref=near_part_ref.at[target],
            dst_ref=near_got_ref.at[source],
            send_sem=near_send.at[target],
            recv_sem=near_recv.at[source],
            device_id=at_near(target),
            device_id_type=MESH,
        )

    def far_copy(source, target, near):
        return pltpu.make_async_remote_copy(
            src_ref=far_part_ref.at[near, target],
            dst_ref=far_got_ref.at[source, near],
            send_sem=far_send.at[near, target],
            recv_sem=far_recv.at[source, near],
            device_id=at_far(target),
            device_id_type=MESH,
        )

    def near_last(source, target):
        return pltpu.make_async_remote_copy(
            src_ref=last_part_ref.at[1, target],
            dst_ref=last_got_ref.at[1, source],
            send_sem=last_send.at[1, target],
            recv_sem=last_recv.at[1, source],
            device_id=at_near(target),
            device_id_type=MESH,
        )

    def far_last(source, target):
        return pltpu.make_async_remote_copy(
            src_ref=last_part_ref.at[0, target],
            dst_ref=last_got_ref.at[0, source],
            send_sem=last_send.at[0, target],
            recv_sem=last_recv.at[0, source],
            device_id=at_far(target),
            device_id_type=MESH,
        )

    for k in range(4):
        sends[k].start()

    code_ref[...] = jnp.zeros_like(code_ref)
    listed = bt_ref[...] + 2048 * bp_ref[...] + (1 << 18) * bs_ref[...]
    code_ref[0:excits, :] = listed.astype(F32)
    own = me_beta * cols + iota((8, cols), 1)
    extra = iota((8, cols), 0)
    own = jnp.where(extra < 2, own + 2048 * (hi_lane + extra) + (1 << 18), 0)
    code_ref[excits : excits + 8, :] = own.astype(F32)
    turned_ref[...] = jnp.zeros_like(turned_ref)
    turned_ref[0:cols, :] = code_ref[...].T
    grouped = turned_ref[pl.ds(0, groups, stride=per_group), :]
    for t in range(1, per_group):
        shifted = turned_ref[pl.ds(t, groups, stride=per_group), :]
        grouped = grouped + pltpu.roll(shifted, t * slots, 1)
    group_ref[...] = grouped.astype(jnp.int32)

    device = at_ref[...] // rows
    near = jnp.bitwise_and(jnp.bitwise_and(device, 3) - place + 3, 3)
    order_ref[...] = (4 * near + device // 4) * rows + jnp.bitwise_and(at_ref[...], rows - 1)

    wide = wide_ref.shape[1]
    arrivals[3].wait_recv()

    def widen(r):
        chip = 2 * turned(here, r)
        for c in range(2):
            wide_ref[r * rows : (r + 1) * rows, c * cols : (c + 1) * cols] = rows_ref[chip + c]

    def pick_code(step):
        coded = [group_ref[pl.ds(2 * step + u, 1), :] for u in range(2)]
        code = jnp.concatenate(coded, axis=1)
        target = jnp.bitwise_and(code, 2047)
        low = jnp.bitwise_and(target, wide - 1)
        sign = (2 * lax.shift_right_logical(code, 18) - 1).astype(F32)
        pick = jnp.where(iota((wide, 2 * LANES), 0) == low, sign, 0.0).astype(BF)
        return jnp.bitwise_and(target // wide - here + chips, chips - 1), pick

    def own_step(step, carry):
        unused, pick = pick_code(step)
        found = jnp.dot(wide_ref[0:rows, :], pick, preferred_element_type=F32).astype(BF)
        for u in range(2):
            own_ref[2 * step + u] = found[:, u * LANES : (u + 1) * LANES]
        return carry

    widen(0)
    lax.fori_loop(0, groups // 2, own_step, 0, unroll=4)

    for k, passed in ((1, 5), (2, 6), (0, 4)):
        arrivals[k].wait_recv()
        sends[passed].start()

    pairs = pair_ref.shape[0]
    one_pad_ref[...] = jnp.zeros_like(one_pad_ref)
    one_pad_ref[0:1, 0:pairs] = one_ref[...]
    pair_pad_ref[...] = jnp.zeros_like(pair_pad_ref)
    pair_pad_ref[0:pairs, 0:pairs] = pair_ref[...].astype(F32)
    one_row = one_pad_ref[0:1, :]
    one_hi = one_row.astype(BF).astype(F32)
    one_lo = one_row - one_hi
    one_two = jnp.concatenate([one_hi, one_lo, jnp.zeros((6, LANES), F32)], axis=0)
    one_cols = jnp.concatenate([one_two, jnp.zeros((LANES - 8, LANES), F32)], axis=0).T
    lane = iota((LANES, LANES), 1)
    table = pair_pad_ref[...]
    table = jnp.where(lane == hi_lane, one_cols[:, 0:1], table)
    table = jnp.where(lane == hi_lane + 1, one_cols[:, 1:2], table)
    table = table.astype(BF)

    def sv_step(e, carry):
        which = ap_ref[pl.ds(e, 1), :]
        sign = (2 * as_ref[pl.ds(e, 1), :] - 1).astype(F32)
        hot = jnp.where(iota((LANES, rows), 0) == which, sign, 0.0).astype(BF)
        sv = lax.dot_general(hot, table, TN, preferred_element_type=F32)
        sv_ref[pl.ds(pl.multiple_of(e * SS, 8), rows), :] = sv
        return carry

    lax.fori_loop(0, excits, sv_step, 0, unroll=8)
    for e, row in enumerate((one_hi, one_lo)):
        start = (excits + e) * SS
        sv_ref[start : start + rows, :] = jnp.broadcast_to(row, (rows, LANES))
    sv_ref[(excits + 2) * SS :, :] = jnp.zeros(((46 - excits) * SS, LANES), F32)

    for k in (5, 6, 4):
        arrivals[k].wait_recv()

    for r in range(1, chips):
        widen(r)
    lane_row = iota((1, LANES), 1)
    lane_slot = lane_row // slots

    def pick_step(step, held, slot):
        block, pick = pick_code(step)
        found = jnp.dot(wide_ref[rows:, :], pick, preferred_element_type=F32)
        picked = jnp.concatenate([own_ref[2 * step + u] for u in range(2)], axis=1).astype(F32)
        for r in range(1, chips):
            picked = jnp.where(block == r, found[(r - 1) * rows : r * rows], picked)
        picked = picked.astype(BF)
        for u in range(2):
            held[2 * slot + u] = picked[:, u * LANES : (u + 1) * LANES]

    def density_step(g, held, slot):
        code = group_ref[pl.ds(g, 1), :]
        pair = jnp.bitwise_and(lax.shift_right_logical(code, 11), 127)
        goal = jnp.where(lane_slot < per_group, lane_slot * LANES + pair, -1)
        spots = iota((per_group * LANES, LANES), 0) == goal
        hot = jnp.where(spots, 1.0, 0.0).astype(BF)
        dens = lax.dot_general(held[slot], hot, NT, preferred_element_type=F32)
        for t in range(per_group):
            base = (per_group * g + t) * DS
            dens_ref[pl.ds(pl.multiple_of(base, 4), rows), :] = dens[
                :, t * LANES : (t + 1) * LANES
            ]

    def both(j, last, held):
        for u in range(BATCH):
            if held is not None:
                pick_step(BATCH * j + u, held, u)
            if last is not None:
                for v in (2 * u, 2 * u + 1):
                    density_step(2 * BATCH * (j - 1) + v, last, v)

    def both_step(k, carry):
        both(2 * k + 1, even_ref, odd_ref)
        both(2 * k + 2, odd_ref, even_ref)
        return carry

    batches = groups // (2 * BATCH)
    both(0, None, even_ref)
    lax.fori_loop(0, (batches - 1) // 2, both_step, 0)
    if batches % 2:
        both(batches, even_ref, None)
    else:
        both(batches - 1, even_ref, odd_ref)
        both(batches, odd_ref, None)

    def lift_step(a, carry):
        weights = sv_ref[pl.ds(a, 48, stride=SS), :].astype(BF)
        dens = dens_ref[pl.ds(a, cols, stride=DS), :].astype(BF)
        out = lax.dot_general(weights, dens, NT, preferred_element_type=F32)
        for half in range(2):
            lift_ref[half, pl.ds(a, 48, stride=LS), :] = out[:, half * LANES : (half + 1) * LANES]
        return carry

    lax.fori_loop(0, rows, lift_step, 0, unroll=16)
    for half in range(2):
        at_half = slice(half * LANES, (half + 1) * LANES)
        for e in range(excits):
            lift_bf_ref[e * rows : (e + 1) * rows, at_half] = lift_ref[
                half, e * LS : e * LS + rows, :
            ].astype(BF)

    tall = 4 * rows

    def spread_step(s, carry):
        hots = []
        for e in range(excits):
            goal = order_ref[e : e + 1, :] - s * tall
            hots.append(jnp.where(iota((tall, rows), 0) == goal, 1.0, 0.0).astype(BF))
        hot = jnp.concatenate(hots, axis=1)
        out = jnp.dot(hot, lift_bf_ref[...], preferred_element_type=F32).astype(BF)
        near = turned(place, s + 1)
        for far in range(4):
            at_rows = slice(far * rows, (far + 1) * rows)
            near_part_ref[near, far] = out[at_rows, 0:LANES]
            far_part_ref[near, far] = out[at_rows, LANES : 2 * LANES]

        @pl.when(s < 3)
        def _():
            near_copy(place, near).start()

        for r in (2, 1, 3):
            far_copy(mine, turned(mine, r), near).start()
        return carry

    lax.fori_loop(0, 4, spread_step, 0)

    for half in range(2):
        at_half = slice(half * LANES, (half + 1) * LANES)
        out_ref[:, at_half] = (
            lift_ref[half, excits * LS : excits * LS + rows, :]
            + lift_ref[half, (excits + 1) * LS : (excits + 1) * LS + rows, :]
        )

    for r in range(1, 4):
        near_copy(turned(place, r), place).wait_recv()
    for r in (2, 1, 3, 0):
        far = turned(mine, r)
        total = near_part_ref[place, far].astype(F32)
        for q in range(1, 4):
            total = total + near_got_ref[turned(place, q), far].astype(F32)
        if r:
            last_part_ref[0, far] = total.astype(BF)
            far_last(mine, far).start()
        else:
            out_ref[:, 0:LANES] = out_ref[:, 0:LANES] + total

    for r in (2, 1, 3, 0):
        near = turned(place, r)
        total = far_part_ref[near, mine].astype(F32)
        for q in range(1, 4):
            source = turned(mine, q)
            far_copy(source, mine, near).wait_recv()
            total = total + far_got_ref[source, near].astype(F32)
        if r:
            last_part_ref[1, near] = total.astype(BF)
            near_last(place, near).start()
        else:
            out_ref[:, LANES : 2 * LANES] = out_ref[:, LANES : 2 * LANES] + total

    total = out_ref[:, 0:LANES]
    for r in range(1, 4):
        far_last(turned(mine, r), mine).wait_recv()
        total = total + last_got_ref[0, turned(mine, r)].astype(F32)
    out_ref[:, 0:LANES] = total
    total = out_ref[:, LANES : 2 * LANES]
    for r in range(1, 4):
        near_last(turned(place, r), place).wait_recv()
        total = total + last_got_ref[1, turned(place, r)].astype(F32)
    out_ref[:, LANES : 2 * LANES] = total

    for copy in sends:
        copy.wait_send()
    for r in range(1, 4):
        near_copy(place, turned(place, r)).wait_send()
        far_last(mine, turned(mine, r)).wait_send()
        near_last(place, turned(place, r)).wait_send()
        for near in range(4):
            far_copy(mine, turned(mine, r), near).wait_send()


def shards(ci_vector, one_body, pair_integrals, bt, bp, bs, at, ap, asg):
    rows, cols = ci_vector.shape
    blocks = lax.axis_size("beta")
    pairs = one_body.shape[0]
    excits = bt.shape[0]
    per_group = LANES // (excits + 2)
    used = -(-cols // per_group)
    groups = -(-used // (2 * BATCH)) * 2 * BATCH
    vmem = pl.BlockSpec(memory_space=pltpu.VMEM)
    return pl.pallas_call(
        functools.partial(compute_kernel, pairs),
        out_shape=jax.ShapeDtypeStruct((rows, cols), F32),
        in_specs=[vmem] * 9,
        out_specs=vmem,
        scratch_shapes=[
            pltpu.VMEM((blocks, rows, cols), BF),
            pltpu.VMEM((4, 4, rows, LANES), BF),
            pltpu.VMEM((4, 4, rows, LANES), BF),
            pltpu.VMEM((4, 4, rows, LANES), BF),
            pltpu.VMEM((4, 4, rows, LANES), BF),
            pltpu.VMEM((2, 4, rows, LANES), BF),
            pltpu.VMEM((2, 4, rows, LANES), BF),
            pltpu.VMEM((8, LANES), F32),
            pltpu.VMEM((LANES, LANES), F32),
            pltpu.VMEM((LANES, cols), F32),
            pltpu.VMEM((groups * per_group, LANES), F32),
            pltpu.VMEM((groups, LANES), jnp.int32),
            pltpu.VMEM((groups * per_group * DS, LANES), F32),
            pltpu.VMEM((48 * SS, LANES), F32),
            pltpu.VMEM((2, 48 * LS, LANES), F32),
            pltpu.VMEM((excits * rows, cols), BF),
            pltpu.VMEM((blocks * rows * cols // WIDE, WIDE), BF),
            pltpu.VMEM((groups, rows, LANES), BF),
            pltpu.VMEM((2 * BATCH, rows, LANES), BF),
            pltpu.VMEM((2 * BATCH, rows, LANES), BF),
            pltpu.VMEM((excits, rows), jnp.int32),
            pltpu.SemaphoreType.DMA((blocks,)),
            pltpu.SemaphoreType.DMA((blocks,)),
            pltpu.SemaphoreType.DMA((4,)),
            pltpu.SemaphoreType.DMA((4,)),
            pltpu.SemaphoreType.DMA((4, 4)),
            pltpu.SemaphoreType.DMA((4, 4)),
            pltpu.SemaphoreType.DMA((2, 4)),
            pltpu.SemaphoreType.DMA((2, 4)),
        ],
        compiler_params=pltpu.CompilerParams(
            vmem_limit_bytes=56 * 2**20, collective_id=0, has_side_effects=True
        ),
    )(ci_vector, one_body.reshape(1, pairs), pair_integrals, bt, bp, bs, at, ap, asg)


def solution(mesh):
    placed = (
        P("alpha", "beta"),
        P(),
        P(),
        P(None, "beta"),
        P(None, "beta"),
        P(None, "beta"),
        P(None, "alpha"),
        P(None, "alpha"),
        P(None, "alpha"),
    )
    return jax.shard_map(
        shards, mesh=mesh, in_specs=placed, out_specs=P("alpha", "beta"), check_vma=False
    )
```

```python
import functools

import jax
import jax.numpy as jnp
from jax import lax
from jax.experimental import pallas as pl
from jax.experimental.pallas import tpu as pltpu
from jax.sharding import PartitionSpec as P

BF = jnp.bfloat16
F32 = jnp.float32
MESH = pl.DeviceIdType.MESH
NT = (((1,), (1,)), ((), ()))
TN = (((0,), (0,)), ((), ()))
LANES = 128
WIDE = 512
DS = 132
SS = 136
LS = 136
BATCH = 4


def iota(shape, dim):
    return lax.broadcasted_iota(jnp.int32, shape, dim)


def compute_kernel(
    hi_lane,
    *refs,
):
    given, refs = refs[:9], refs[9:]
    (
        out_ref,
        rows_ref,
        near_part_ref,
        far_part_ref,
        near_got_ref,
        far_got_ref,
        last_part_ref,
        last_got_ref,
        one_pad_ref,
        pair_pad_ref,
        code_ref,
        turned_ref,
        group_ref,
        dens_ref,
        sv_ref,
        lift_ref,
        lift_bf_ref,
        wide_ref,
        own_ref,
        even_ref,
        odd_ref,
        order_ref,
        beta_send,
        beta_recv,
        near_send,
        near_recv,
        far_send,
        far_recv,
        last_send,
        last_recv,
        ci_ref,
        one_ref,
        pair_ref,
        bt_ref,
        bp_ref,
        bs_ref,
        at_ref,
        ap_ref,
        as_ref,
        load_sem,
    ) = refs
    blocks, rows, cols = rows_ref.shape
    excits = bt_ref.shape[0]
    slots = excits + 2
    per_group = LANES // slots
    groups = group_ref.shape[0]
    me_beta = lax.axis_index("beta")
    me_alpha = lax.axis_index("alpha")

    barrier = pltpu.get_barrier_semaphore()
    chips = blocks // 2
    here, core = me_beta // 2, lax.rem(me_beta, 2)
    sibling = 2 * here + 1 - core
    right = 2 * lax.rem(here + 1, chips) + core
    left = 2 * lax.rem(here + chips - 1, chips) + core
    across = 2 * lax.rem(here + 2, chips) + core
    beta_peers = (sibling, left, right, across)
    for peer in beta_peers:
        pl.semaphore_signal(barrier, inc=1, device_id={"beta": peer}, device_id_type=MESH)
    mine, place = me_alpha // 4, lax.rem(me_alpha, 4)

    def at_far(far):
        return {"alpha": 4 * far + place}

    def at_near(near):
        return {"alpha": 4 * mine + near}

    def turned(start, r):
        return lax.rem(start + r, 4)

    for r in range(1, 4):
        for peer in (at_far(turned(mine, r)), at_near(turned(place, r))):
            pl.semaphore_signal(barrier, inc=1, device_id=peer, device_id_type=MESH)
    kept = (ci_ref, bt_ref, bp_ref, bs_ref, at_ref, ap_ref, as_ref, one_ref, pair_ref)
    order = (0, 3, 4, 5, 6, 7, 8, 1, 2)
    loads = [
        pltpu.make_async_copy(given[n], kept[k], load_sem.at[k]) for k, n in enumerate(order)
    ]
    for load in loads:
        load.start()
    loads[0].wait()
    rows_ref[me_beta] = ci_ref[...].astype(BF)
    pl.semaphore_wait(barrier, len(beta_peers) + 6)

    def row_copy(k, block, target):
        return pltpu.make_async_remote_copy(
            src_ref=rows_ref.at[block],
            dst_ref=rows_ref.at[block],
            send_sem=beta_send.at[k],
            recv_sem=beta_recv.at[k],
            device_id={"beta": target},
            device_id_type=MESH,
        )

    def other(block):
        return block + 1 - 2 * core

    sends = [
        row_copy(0, me_beta, across),
        row_copy(1, me_beta, right),
        row_copy(2, me_beta, left),
        row_copy(3, me_beta, sibling),
        row_copy(4, across, sibling),
        row_copy(5, left, sibling),
        row_copy(6, right, sibling),
    ]
    arrivals = [
        row_copy(0, across, me_beta),
        row_copy(1, left, me_beta),
        row_copy(2, right, me_beta),
        row_copy(3, sibling, me_beta),
        row_copy(4, other(across), me_beta),
        row_copy(5, other(left), me_beta),
        row_copy(6, other(right), me_beta),
    ]

    def near_copy(source, target):
        return pltpu.make_async_remote_copy(
            src_ref=near_part_ref.at[target],
            dst_ref=near_got_ref.at[source],
            send_sem=near_send.at[target],
            recv_sem=near_recv.at[source],
            device_id=at_near(target),
            device_id_type=MESH,
        )

    def far_copy(source, target, near):
        return pltpu.make_async_remote_copy(
            src_ref=far_part_ref.at[near, target],
            dst_ref=far_got_ref.at[source, near],
            send_sem=far_send.at[near, target],
            recv_sem=far_recv.at[source, near],
            device_id=at_far(target),
            device_id_type=MESH,
        )

    def near_last(source, target):
        return pltpu.make_async_remote_copy(
            src_ref=last_part_ref.at[1, target],
            dst_ref=last_got_ref.at[1, source],
            send_sem=last_send.at[1, target],
            recv_sem=last_recv.at[1, source],
            device_id=at_near(target),
            device_id_type=MESH,
        )

    def far_last(source, target):
        return pltpu.make_async_remote_copy(
            src_ref=last_part_ref.at[0, target],
            dst_ref=last_got_ref.at[0, source],
            send_sem=last_send.at[0, target],
            recv_sem=last_recv.at[0, source],
            device_id=at_far(target),
            device_id_type=MESH,
        )

    for k in range(4):
        sends[k].start()

    for load in loads[1:]:
        load.wait()

    code_ref[...] = jnp.zeros_like(code_ref)
    listed = bt_ref[...] + 2048 * bp_ref[...] + (1 << 18) * bs_ref[...]
    code_ref[0:excits, :] = listed.astype(F32)
    own = me_beta * cols + iota((8, cols), 1)
    extra = iota((8, cols), 0)
    own = jnp.where(extra < 2, own + 2048 * (hi_lane + extra) + (1 << 18), 0)
    code_ref[excits : excits + 8, :] = own.astype(F32)
    turned_ref[...] = jnp.zeros_like(turned_ref)
    turned_ref[0:cols, :] = code_ref[...].T
    grouped = turned_ref[pl.ds(0, groups, stride=per_group), :]
    for t in range(1, per_group):
        shifted = turned_ref[pl.ds(t, groups, stride=per_group), :]
        grouped = grouped + pltpu.roll(shifted, t * slots, 1)
    group_ref[...] = grouped.astype(jnp.int32)

    device = at_ref[...] // rows
    near = jnp.bitwise_and(jnp.bitwise_and(device, 3) - place + 3, 3)
    order_ref[...] = (4 * near + device // 4) * rows + jnp.bitwise_and(at_ref[...], rows - 1)

    wide = wide_ref.shape[1]
    arrivals[3].wait_recv()

    def widen(r):
        chip = 2 * turned(here, r)
        for c in range(2):
            wide_ref[r * rows : (r + 1) * rows, c * cols : (c + 1) * cols] = rows_ref[chip + c]

    def pick_code(step):
        coded = [group_ref[pl.ds(2 * step + u, 1), :] for u in range(2)]
        code = jnp.concatenate(coded, axis=1)
        target = jnp.bitwise_and(code, 2047)
        low = jnp.bitwise_and(target, wide - 1)
        sign = (2 * lax.shift_right_logical(code, 18) - 1).astype(F32)
        pick = jnp.where(iota((wide, 2 * LANES), 0) == low, sign, 0.0).astype(BF)
        return jnp.bitwise_and(target // wide - here + chips, chips - 1), pick

    def own_step(step, carry):
        unused, pick = pick_code(step)
        found = jnp.dot(wide_ref[0:rows, :], pick, preferred_element_type=F32).astype(BF)
        for u in range(2):
            own_ref[2 * step + u] = found[:, u * LANES : (u + 1) * LANES]
        return carry

    widen(0)
    lax.fori_loop(0, groups // 2, own_step, 0, unroll=4)

    for k, passed in ((1, 5), (2, 6), (0, 4)):
        arrivals[k].wait_recv()
        sends[passed].start()

    pairs = pair_ref.shape[0]
    one_pad_ref[...] = jnp.zeros_like(one_pad_ref)
    one_pad_ref[0:1, 0:pairs] = one_ref[...]
    pair_pad_ref[...] = jnp.zeros_like(pair_pad_ref)
    pair_pad_ref[0:pairs, 0:pairs] = pair_ref[...].astype(F32)
    one_row = one_pad_ref[0:1, :]
    one_hi = one_row.astype(BF).astype(F32)
    one_lo = one_row - one_hi
    one_two = jnp.concatenate([one_hi, one_lo, jnp.zeros((6, LANES), F32)], axis=0)
    one_cols = jnp.concatenate([one_two, jnp.zeros((LANES - 8, LANES), F32)], axis=0).T
    lane = iota((LANES, LANES), 1)
    table = pair_pad_ref[...]
    table = jnp.where(lane == hi_lane, one_cols[:, 0:1], table)
    table = jnp.where(lane == hi_lane + 1, one_cols[:, 1:2], table)
    table = table.astype(BF)

    def sv_step(e, carry):
        which = ap_ref[pl.ds(e, 1), :]
        sign = (2 * as_ref[pl.ds(e, 1), :] - 1).astype(F32)
        hot = jnp.where(iota((LANES, rows), 0) == which, sign, 0.0).astype(BF)
        sv = lax.dot_general(hot, table, TN, preferred_element_type=F32)
        sv_ref[pl.ds(pl.multiple_of(e * SS, 8), rows), :] = sv
        return carry

    lax.fori_loop(0, excits, sv_step, 0, unroll=8)
    for e, row in enumerate((one_hi, one_lo)):
        start = (excits + e) * SS
        sv_ref[start : start + rows, :] = jnp.broadcast_to(row, (rows, LANES))
    sv_ref[(excits + 2) * SS :, :] = jnp.zeros(((46 - excits) * SS, LANES), F32)

    for k in (5, 6, 4):
        arrivals[k].wait_recv()

    for r in range(1, chips):
        widen(r)
    lane_row = iota((1, LANES), 1)
    lane_slot = lane_row // slots

    def pick_step(step, held, slot):
        block, pick = pick_code(step)
        found = jnp.dot(wide_ref[rows:, :], pick, preferred_element_type=F32)
        picked = jnp.concatenate([own_ref[2 * step + u] for u in range(2)], axis=1).astype(F32)
        for r in range(1, chips):
            picked = jnp.where(block == r, found[(r - 1) * rows : r * rows], picked)
        picked = picked.astype(BF)
        for u in range(2):
            held[2 * slot + u] = picked[:, u * LANES : (u + 1) * LANES]

    def density_step(g, held, slot):
        code = group_ref[pl.ds(g, 1), :]
        pair = jnp.bitwise_and(lax.shift_right_logical(code, 11), 127)
        goal = jnp.where(lane_slot < per_group, lane_slot * LANES + pair, -1)
        spots = iota((per_group * LANES, LANES), 0) == goal
        hot = jnp.where(spots, 1.0, 0.0).astype(BF)
        dens = lax.dot_general(held[slot], hot, NT, preferred_element_type=F32)
        for t in range(per_group):
            base = (per_group * g + t) * DS
            dens_ref[pl.ds(pl.multiple_of(base, 4), rows), :] = dens[
                :, t * LANES : (t + 1) * LANES
            ]

    def both(j, last, held):
        for u in range(BATCH):
            if held is not None:
                pick_step(BATCH * j + u, held, u)
            if last is not None:
                for v in (2 * u, 2 * u + 1):
                    density_step(2 * BATCH * (j - 1) + v, last, v)

    def both_step(k, carry):
        both(2 * k + 1, even_ref, odd_ref)
        both(2 * k + 2, odd_ref, even_ref)
        return carry

    batches = groups // (2 * BATCH)
    both(0, None, even_ref)
    lax.fori_loop(0, (batches - 1) // 2, both_step, 0)
    if batches % 2:
        both(batches, even_ref, None)
    else:
        both(batches - 1, even_ref, odd_ref)
        both(batches, odd_ref, None)

    def lift_step(a, carry):
        weights = sv_ref[pl.ds(a, 48, stride=SS), :].astype(BF)
        dens = dens_ref[pl.ds(a, cols, stride=DS), :].astype(BF)
        out = lax.dot_general(weights, dens, NT, preferred_element_type=F32)
        for half in range(2):
            lift_ref[half, pl.ds(a, 48, stride=LS), :] = out[:, half * LANES : (half + 1) * LANES]
        return carry

    lax.fori_loop(0, rows, lift_step, 0, unroll=32)
    for half in range(2):
        at_half = slice(half * LANES, (half + 1) * LANES)
        for e in range(excits):
            lift_bf_ref[e * rows : (e + 1) * rows, at_half] = lift_ref[
                half, e * LS : e * LS + rows, :
            ].astype(BF)

    tall = 4 * rows

    def spread_step(s, carry):
        hots = []
        for e in range(excits):
            goal = order_ref[e : e + 1, :] - s * tall
            hots.append(jnp.where(iota((tall, rows), 0) == goal, 1.0, 0.0).astype(BF))
        hot = jnp.concatenate(hots, axis=1)
        out = jnp.dot(hot, lift_bf_ref[...], preferred_element_type=F32).astype(BF)
        near = turned(place, s + 1)
        for far in range(4):
            at_rows = slice(far * rows, (far + 1) * rows)
            near_part_ref[near, far] = out[at_rows, 0:LANES]
            far_part_ref[near, far] = out[at_rows, LANES : 2 * LANES]

        @pl.when(s < 3)
        def _():
            near_copy(place, near).start()

        for r in (2, 1, 3):
            far_copy(mine, turned(mine, r), near).start()
        return carry

    lax.fori_loop(0, 4, spread_step, 0)

    for half in range(2):
        at_half = slice(half * LANES, (half + 1) * LANES)
        out_ref[:, at_half] = (
            lift_ref[half, excits * LS : excits * LS + rows, :]
            + lift_ref[half, (excits + 1) * LS : (excits + 1) * LS + rows, :]
        )

    for r in range(1, 4):
        near_copy(turned(place, r), place).wait_recv()
    for r in (2, 1, 3, 0):
        far = turned(mine, r)
        total = near_part_ref[place, far].astype(F32)
        for q in range(1, 4):
            total = total + near_got_ref[turned(place, q), far].astype(F32)
        if r:
            last_part_ref[0, far] = total.astype(BF)
            far_last(mine, far).start()
        else:
            out_ref[:, 0:LANES] = out_ref[:, 0:LANES] + total

    for r in (2, 1, 3, 0):
        near = turned(place, r)
        total = far_part_ref[near, mine].astype(F32)
        for q in range(1, 4):
            source = turned(mine, q)
            far_copy(source, mine, near).wait_recv()
            total = total + far_got_ref[source, near].astype(F32)
        if r:
            last_part_ref[1, near] = total.astype(BF)
            near_last(place, near).start()
        else:
            out_ref[:, LANES : 2 * LANES] = out_ref[:, LANES : 2 * LANES] + total

    total = out_ref[:, 0:LANES]
    for r in range(1, 4):
        far_last(turned(mine, r), mine).wait_recv()
        total = total + last_got_ref[0, turned(mine, r)].astype(F32)
    out_ref[:, 0:LANES] = total
    total = out_ref[:, LANES : 2 * LANES]
    for r in range(1, 4):
        near_last(turned(place, r), place).wait_recv()
        total = total + last_got_ref[1, turned(place, r)].astype(F32)
    out_ref[:, LANES : 2 * LANES] = total

    for copy in sends:
        copy.wait_send()
    for r in range(1, 4):
        near_copy(place, turned(place, r)).wait_send()
        far_last(mine, turned(mine, r)).wait_send()
        near_last(place, turned(place, r)).wait_send()
        for near in range(4):
            far_copy(mine, turned(mine, r), near).wait_send()


def shards(ci_vector, one_body, pair_integrals, bt, bp, bs, at, ap, asg):
    rows, cols = ci_vector.shape
    blocks = lax.axis_size("beta")
    pairs = one_body.shape[0]
    excits = bt.shape[0]
    per_group = LANES // (excits + 2)
    used = -(-cols // per_group)
    groups = -(-used // (2 * BATCH)) * 2 * BATCH
    vmem = pl.BlockSpec(memory_space=pltpu.VMEM)
    return pl.pallas_call(
        functools.partial(compute_kernel, pairs),
        out_shape=jax.ShapeDtypeStruct((rows, cols), F32),
        in_specs=[pl.BlockSpec(memory_space=pltpu.HBM)] * 9,
        out_specs=vmem,
        scratch_shapes=[
            pltpu.VMEM((blocks, rows, cols), BF),
            pltpu.VMEM((4, 4, rows, LANES), BF),
            pltpu.VMEM((4, 4, rows, LANES), BF),
            pltpu.VMEM((4, 4, rows, LANES), BF),
            pltpu.VMEM((4, 4, rows, LANES), BF),
            pltpu.VMEM((2, 4, rows, LANES), BF),
            pltpu.VMEM((2, 4, rows, LANES), BF),
            pltpu.VMEM((8, LANES), F32),
            pltpu.VMEM((LANES, LANES), F32),
            pltpu.VMEM((LANES, cols), F32),
            pltpu.VMEM((groups * per_group, LANES), F32),
            pltpu.VMEM((groups, LANES), jnp.int32),
            pltpu.VMEM((groups * per_group * DS, LANES), F32),
            pltpu.VMEM((48 * SS, LANES), F32),
            pltpu.VMEM((2, 48 * LS, LANES), F32),
            pltpu.VMEM((excits * rows, cols), BF),
            pltpu.VMEM((blocks * rows * cols // WIDE, WIDE), BF),
            pltpu.VMEM((groups, rows, LANES), BF),
            pltpu.VMEM((2 * BATCH, rows, LANES), BF),
            pltpu.VMEM((2 * BATCH, rows, LANES), BF),
            pltpu.VMEM((excits, rows), jnp.int32),
            pltpu.SemaphoreType.DMA((blocks,)),
            pltpu.SemaphoreType.DMA((blocks,)),
            pltpu.SemaphoreType.DMA((4,)),
            pltpu.SemaphoreType.DMA((4,)),
            pltpu.SemaphoreType.DMA((4, 4)),
            pltpu.SemaphoreType.DMA((4, 4)),
            pltpu.SemaphoreType.DMA((2, 4)),
            pltpu.SemaphoreType.DMA((2, 4)),
            pltpu.VMEM((rows, cols), F32),
            pltpu.VMEM((1, pairs), F32),
            pltpu.VMEM((pairs, pairs), BF),
            pltpu.VMEM((excits, cols), jnp.int32),
            pltpu.VMEM((excits, cols), jnp.int32),
            pltpu.VMEM((excits, cols), jnp.int32),
            pltpu.VMEM((excits, rows), jnp.int32),
            pltpu.VMEM((excits, rows), jnp.int32),
            pltpu.VMEM((excits, rows), jnp.int32),
            pltpu.SemaphoreType.DMA((9,)),
        ],
        compiler_params=pltpu.CompilerParams(
            vmem_limit_bytes=56 * 2**20, collective_id=0, has_side_effects=True
        ),
    )(ci_vector, one_body.reshape(1, pairs), pair_integrals, bt, bp, bs, at, ap, asg)


def solution(mesh):
    placed = (
        P("alpha", "beta"),
        P(),
        P(),
        P(None, "beta"),
        P(None, "beta"),
        P(None, "beta"),
        P(None, "alpha"),
        P(None, "alpha"),
        P(None, "alpha"),
    )
    return jax.shard_map(
        shards, mesh=mesh, in_specs=placed, out_specs=P("alpha", "beta"), check_vma=False
    )
```

```python
import functools

import jax
import jax.numpy as jnp
from jax import lax
from jax.experimental import pallas as pl
from jax.experimental.pallas import tpu as pltpu
from jax.sharding import PartitionSpec as P

BF = jnp.bfloat16
F32 = jnp.float32
MESH = pl.DeviceIdType.MESH
NT = (((1,), (1,)), ((), ()))
TN = (((0,), (0,)), ((), ()))
LANES = 128
WIDE = 512
DS = 132
SS = 136
LS = 136
BATCH = 11


def iota(shape, dim):
    return lax.broadcasted_iota(jnp.int32, shape, dim)


def compute_kernel(
    hi_lane,
    *refs,
):
    given, refs = refs[:9], refs[9:]
    (
        out_ref,
        rows_ref,
        near_part_ref,
        far_part_ref,
        near_got_ref,
        far_got_ref,
        last_part_ref,
        last_got_ref,
        one_pad_ref,
        pair_pad_ref,
        code_ref,
        turned_ref,
        group_ref,
        dens_ref,
        sv_ref,
        lift_ref,
        lift_bf_ref,
        wide_ref,
        own_ref,
        even_ref,
        odd_ref,
        order_ref,
        beta_send,
        beta_recv,
        near_send,
        near_recv,
        far_send,
        far_recv,
        last_send,
        last_recv,
        ci_ref,
        one_ref,
        pair_ref,
        bt_ref,
        bp_ref,
        bs_ref,
        at_ref,
        ap_ref,
        as_ref,
        load_sem,
    ) = refs
    blocks, rows, cols = rows_ref.shape
    excits = bt_ref.shape[0]
    slots = excits + 2
    per_group = LANES // slots
    groups = group_ref.shape[0]
    me_beta = lax.axis_index("beta")
    me_alpha = lax.axis_index("alpha")

    barrier = pltpu.get_barrier_semaphore()
    chips = blocks // 2
    here, core = me_beta // 2, lax.rem(me_beta, 2)
    sibling = 2 * here + 1 - core
    right = 2 * lax.rem(here + 1, chips) + core
    left = 2 * lax.rem(here + chips - 1, chips) + core
    across = 2 * lax.rem(here + 2, chips) + core
    beta_peers = (sibling, left, right, across)
    for peer in beta_peers:
        pl.semaphore_signal(barrier, inc=1, device_id={"beta": peer}, device_id_type=MESH)
    mine, place = me_alpha // 4, lax.rem(me_alpha, 4)

    def at_far(far):
        return {"alpha": 4 * far + place}

    def at_near(near):
        return {"alpha": 4 * mine + near}

    def turned(start, r):
        return lax.rem(start + r, 4)

    for r in range(1, 4):
        for peer in (at_far(turned(mine, r)), at_near(turned(place, r))):
            pl.semaphore_signal(barrier, inc=1, device_id=peer, device_id_type=MESH)
    kept = (ci_ref, bt_ref, bp_ref, bs_ref, at_ref, ap_ref, as_ref, one_ref, pair_ref)
    order = (0, 3, 4, 5, 6, 7, 8, 1, 2)
    loads = [
        pltpu.make_async_copy(given[n], kept[k], load_sem.at[k]) for k, n in enumerate(order)
    ]
    for load in loads:
        load.start()
    loads[0].wait()
    rows_ref[me_beta] = ci_ref[...].astype(BF)
    pl.semaphore_wait(barrier, len(beta_peers) + 6)

    def row_copy(k, block, target):
        return pltpu.make_async_remote_copy(
            src_ref=rows_ref.at[block],
            dst_ref=rows_ref.at[block],
            send_sem=beta_send.at[k],
            recv_sem=beta_recv.at[k],
            device_id={"beta": target},
            device_id_type=MESH,
        )

    def other(block):
        return block + 1 - 2 * core

    sends = [
        row_copy(0, me_beta, across),
        row_copy(1, me_beta, right),
        row_copy(2, me_beta, left),
        row_copy(3, me_beta, sibling),
        row_copy(4, across, sibling),
        row_copy(5, left, sibling),
        row_copy(6, right, sibling),
    ]
    arrivals = [
        row_copy(0, across, me_beta),
        row_copy(1, left, me_beta),
        row_copy(2, right, me_beta),
        row_copy(3, sibling, me_beta),
        row_copy(4, other(across), me_beta),
        row_copy(5, other(left), me_beta),
        row_copy(6, other(right), me_beta),
    ]

    def near_copy(source, target):
        return pltpu.make_async_remote_copy(
            src_ref=near_part_ref.at[target],
            dst_ref=near_got_ref.at[source],
            send_sem=near_send.at[target],
            recv_sem=near_recv.at[source],
            device_id=at_near(target),
            device_id_type=MESH,
        )

    def far_copy(source, target, near):
        return pltpu.make_async_remote_copy(
            src_ref=far_part_ref.at[near, target],
            dst_ref=far_got_ref.at[source, near],
            send_sem=far_send.at[near, target],
            recv_sem=far_recv.at[source, near],
            device_id=at_far(target),
            device_id_type=MESH,
        )

    def near_last(source, target):
        return pltpu.make_async_remote_copy(
            src_ref=last_part_ref.at[1, target],
            dst_ref=last_got_ref.at[1, source],
            send_sem=last_send.at[1, target],
            recv_sem=last_recv.at[1, source],
            device_id=at_near(target),
            device_id_type=MESH,
        )

    def far_last(source, target):
        return pltpu.make_async_remote_copy(
            src_ref=last_part_ref.at[0, target],
            dst_ref=last_got_ref.at[0, source],
            send_sem=last_send.at[0, target],
            recv_sem=last_recv.at[0, source],
            device_id=at_far(target),
            device_id_type=MESH,
        )

    for k in range(4):
        sends[k].start()

    for load in loads[1:]:
        load.wait()

    code_ref[...] = jnp.zeros_like(code_ref)
    listed = bt_ref[...] + 2048 * bp_ref[...] + (1 << 18) * bs_ref[...]
    code_ref[0:excits, :] = listed.astype(F32)
    own = me_beta * cols + iota((8, cols), 1)
    extra = iota((8, cols), 0)
    own = jnp.where(extra < 2, own + 2048 * (hi_lane + extra) + (1 << 18), 0)
    code_ref[excits : excits + 8, :] = own.astype(F32)
    turned_ref[...] = jnp.zeros_like(turned_ref)
    turned_ref[0:cols, :] = code_ref[...].T
    grouped = turned_ref[pl.ds(0, groups, stride=per_group), :]
    for t in range(1, per_group):
        shifted = turned_ref[pl.ds(t, groups, stride=per_group), :]
        grouped = grouped + pltpu.roll(shifted, t * slots, 1)
    group_ref[...] = grouped.astype(jnp.int32)

    device = at_ref[...] // rows
    near = jnp.bitwise_and(jnp.bitwise_and(device, 3) - place + 3, 3)
    order_ref[...] = (4 * near + device // 4) * rows + jnp.bitwise_and(at_ref[...], rows - 1)

    wide = wide_ref.shape[1]
    arrivals[3].wait_recv()

    def widen(r):
        chip = 2 * turned(here, r)
        for c in range(2):
            wide_ref[r * rows : (r + 1) * rows, c * cols : (c + 1) * cols] = rows_ref[chip + c]

    def pick_code(step):
        coded = [group_ref[pl.ds(2 * step + u, 1), :] for u in range(2)]
        code = jnp.concatenate(coded, axis=1)
        target = jnp.bitwise_and(code, 2047)
        low = jnp.bitwise_and(target, wide - 1)
        sign = (2 * lax.shift_right_logical(code, 18) - 1).astype(F32)
        pick = jnp.where(iota((wide, 2 * LANES), 0) == low, sign, 0.0).astype(BF)
        return jnp.bitwise_and(target // wide - here + chips, chips - 1), pick

    def own_step(step, carry):
        unused, pick = pick_code(step)
        found = jnp.dot(wide_ref[0:rows, :], pick, preferred_element_type=F32).astype(BF)
        for u in range(2):
            own_ref[2 * step + u] = found[:, u * LANES : (u + 1) * LANES]
        return carry

    widen(0)
    lax.fori_loop(0, groups // 2, own_step, 0, unroll=4)

    for k, passed in ((1, 5), (2, 6), (0, 4)):
        arrivals[k].wait_recv()
        sends[passed].start()

    pairs = pair_ref.shape[0]
    one_pad_ref[...] = jnp.zeros_like(one_pad_ref)
    one_pad_ref[0:1, 0:pairs] = one_ref[...]
    pair_pad_ref[...] = jnp.zeros_like(pair_pad_ref)
    pair_pad_ref[0:pairs, 0:pairs] = pair_ref[...].astype(F32)
    one_row = one_pad_ref[0:1, :]
    one_hi = one_row.astype(BF).astype(F32)
    one_lo = one_row - one_hi
    one_two = jnp.concatenate([one_hi, one_lo, jnp.zeros((6, LANES), F32)], axis=0)
    one_cols = jnp.concatenate([one_two, jnp.zeros((LANES - 8, LANES), F32)], axis=0).T
    lane = iota((LANES, LANES), 1)
    table = pair_pad_ref[...]
    table = jnp.where(lane == hi_lane, one_cols[:, 0:1], table)
    table = jnp.where(lane == hi_lane + 1, one_cols[:, 1:2], table)
    table = table.astype(BF)

    def sv_step(e, carry):
        which = ap_ref[pl.ds(e, 1), :]
        sign = (2 * as_ref[pl.ds(e, 1), :] - 1).astype(F32)
        hot = jnp.where(iota((LANES, rows), 0) == which, sign, 0.0).astype(BF)
        sv = lax.dot_general(hot, table, TN, preferred_element_type=F32)
        sv_ref[pl.ds(pl.multiple_of(e * SS, 8), rows), :] = sv
        return carry

    lax.fori_loop(0, excits, sv_step, 0, unroll=8)
    for e, row in enumerate((one_hi, one_lo)):
        start = (excits + e) * SS
        sv_ref[start : start + rows, :] = jnp.broadcast_to(row, (rows, LANES))
    sv_ref[(excits + 2) * SS :, :] = jnp.zeros(((46 - excits) * SS, LANES), F32)

    for k in (5, 6, 4):
        arrivals[k].wait_recv()

    for r in range(1, chips):
        widen(r)
    lane_row = iota((1, LANES), 1)
    lane_slot = lane_row // slots

    def pick_step(step, held, slot):
        block, pick = pick_code(step)
        found = jnp.dot(wide_ref[rows:, :], pick, preferred_element_type=F32)
        picked = jnp.concatenate([own_ref[2 * step + u] for u in range(2)], axis=1).astype(F32)
        for r in range(1, chips):
            picked = jnp.where(block == r, found[(r - 1) * rows : r * rows], picked)
        picked = picked.astype(BF)
        for u in range(2):
            held[2 * slot + u] = picked[:, u * LANES : (u + 1) * LANES]

    def density_step(g, held, slot):
        code = group_ref[pl.ds(g, 1), :]
        pair = jnp.bitwise_and(lax.shift_right_logical(code, 11), 127)
        goal = jnp.where(lane_slot < per_group, lane_slot * LANES + pair, -1)
        spots = iota((per_group * LANES, LANES), 0) == goal
        hot = jnp.where(spots, 1.0, 0.0).astype(BF)
        dens = lax.dot_general(held[slot], hot, NT, preferred_element_type=F32)
        for t in range(per_group):
            base = (per_group * g + t) * DS
            dens_ref[pl.ds(pl.multiple_of(base, 4), rows), :] = dens[
                :, t * LANES : (t + 1) * LANES
            ]

    def both(j, last, held):
        for u in range(BATCH):
            if held is not None:
                pick_step(BATCH * j + u, held, u)
            if last is not None:
                for v in (2 * u, 2 * u + 1):
                    density_step(2 * BATCH * (j - 1) + v, last, v)

    def both_step(k, carry):
        both(2 * k + 1, even_ref, odd_ref)
        both(2 * k + 2, odd_ref, even_ref)
        return carry

    batches = groups // (2 * BATCH)
    both(0, None, even_ref)
    lax.fori_loop(0, (batches - 1) // 2, both_step, 0)
    if batches % 2:
        both(batches, even_ref, None)
    else:
        both(batches - 1, even_ref, odd_ref)
        both(batches, odd_ref, None)

    def lift_step(a, carry):
        weights = sv_ref[pl.ds(a, 48, stride=SS), :].astype(BF)
        dens = dens_ref[pl.ds(a, cols, stride=DS), :].astype(BF)
        out = lax.dot_general(weights, dens, NT, preferred_element_type=F32)
        for half in range(2):
            lift_ref[half, pl.ds(a, 48, stride=LS), :] = out[:, half * LANES : (half + 1) * LANES]
        return carry

    lax.fori_loop(0, rows, lift_step, 0, unroll=32)
    for half in range(2):
        at_half = slice(half * LANES, (half + 1) * LANES)
        for e in range(excits):
            lift_bf_ref[e * rows : (e + 1) * rows, at_half] = lift_ref[
                half, e * LS : e * LS + rows, :
            ].astype(BF)

    tall = 4 * rows

    def spread_step(s, carry):
        hots = []
        for e in range(excits):
            goal = order_ref[e : e + 1, :] - s * tall
            hots.append(jnp.where(iota((tall, rows), 0) == goal, 1.0, 0.0).astype(BF))
        hot = jnp.concatenate(hots, axis=1)
        out = jnp.dot(hot, lift_bf_ref[...], preferred_element_type=F32).astype(BF)
        near = turned(place, s + 1)
        for far in range(4):
            at_rows = slice(far * rows, (far + 1) * rows)
            near_part_ref[near, far] = out[at_rows, 0:LANES]
            far_part_ref[near, far] = out[at_rows, LANES : 2 * LANES]

        @pl.when(s < 3)
        def _():
            near_copy(place, near).start()

        for r in (2, 1, 3):
            far_copy(mine, turned(mine, r), near).start()
        return carry

    lax.fori_loop(0, 4, spread_step, 0)

    for half in range(2):
        at_half = slice(half * LANES, (half + 1) * LANES)
        out_ref[:, at_half] = (
            lift_ref[half, excits * LS : excits * LS + rows, :]
            + lift_ref[half, (excits + 1) * LS : (excits + 1) * LS + rows, :]
        )

    for r in range(1, 4):
        near_copy(turned(place, r), place).wait_recv()
    for r in (2, 1, 3, 0):
        far = turned(mine, r)
        total = near_part_ref[place, far].astype(F32)
        for q in range(1, 4):
            total = total + near_got_ref[turned(place, q), far].astype(F32)
        if r:
            last_part_ref[0, far] = total.astype(BF)
            far_last(mine, far).start()
        else:
            out_ref[:, 0:LANES] = out_ref[:, 0:LANES] + total

    for r in (2, 1, 3, 0):
        near = turned(place, r)
        total = far_part_ref[near, mine].astype(F32)
        for q in range(1, 4):
            source = turned(mine, q)
            far_copy(source, mine, near).wait_recv()
            total = total + far_got_ref[source, near].astype(F32)
        if r:
            last_part_ref[1, near] = total.astype(BF)
            near_last(place, near).start()
        else:
            out_ref[:, LANES : 2 * LANES] = out_ref[:, LANES : 2 * LANES] + total

    total = out_ref[:, 0:LANES]
    for r in range(1, 4):
        far_last(turned(mine, r), mine).wait_recv()
        total = total + last_got_ref[0, turned(mine, r)].astype(F32)
    out_ref[:, 0:LANES] = total
    total = out_ref[:, LANES : 2 * LANES]
    for r in range(1, 4):
        near_last(turned(place, r), place).wait_recv()
        total = total + last_got_ref[1, turned(place, r)].astype(F32)
    out_ref[:, LANES : 2 * LANES] = total

    for copy in sends:
        copy.wait_send()
    for r in range(1, 4):
        near_copy(place, turned(place, r)).wait_send()
        far_last(mine, turned(mine, r)).wait_send()
        near_last(place, turned(place, r)).wait_send()
        for near in range(4):
            far_copy(mine, turned(mine, r), near).wait_send()


def shards(ci_vector, one_body, pair_integrals, bt, bp, bs, at, ap, asg):
    rows, cols = ci_vector.shape
    blocks = lax.axis_size("beta")
    pairs = one_body.shape[0]
    excits = bt.shape[0]
    per_group = LANES // (excits + 2)
    used = -(-cols // per_group)
    groups = -(-used // (2 * BATCH)) * 2 * BATCH
    vmem = pl.BlockSpec(memory_space=pltpu.VMEM)
    return pl.pallas_call(
        functools.partial(compute_kernel, pairs),
        out_shape=jax.ShapeDtypeStruct((rows, cols), F32),
        in_specs=[pl.BlockSpec(memory_space=pltpu.HBM)] * 9,
        out_specs=vmem,
        scratch_shapes=[
            pltpu.VMEM((blocks, rows, cols), BF),
            pltpu.VMEM((4, 4, rows, LANES), BF),
            pltpu.VMEM((4, 4, rows, LANES), BF),
            pltpu.VMEM((4, 4, rows, LANES), BF),
            pltpu.VMEM((4, 4, rows, LANES), BF),
            pltpu.VMEM((2, 4, rows, LANES), BF),
            pltpu.VMEM((2, 4, rows, LANES), BF),
            pltpu.VMEM((8, LANES), F32),
            pltpu.VMEM((LANES, LANES), F32),
            pltpu.VMEM((LANES, cols), F32),
            pltpu.VMEM((groups * per_group, LANES), F32),
            pltpu.VMEM((groups, LANES), jnp.int32),
            pltpu.VMEM((groups * per_group * DS, LANES), F32),
            pltpu.VMEM((48 * SS, LANES), F32),
            pltpu.VMEM((2, 48 * LS, LANES), F32),
            pltpu.VMEM((excits * rows, cols), BF),
            pltpu.VMEM((blocks * rows * cols // WIDE, WIDE), BF),
            pltpu.VMEM((groups, rows, LANES), BF),
            pltpu.VMEM((2 * BATCH, rows, LANES), BF),
            pltpu.VMEM((2 * BATCH, rows, LANES), BF),
            pltpu.VMEM((excits, rows), jnp.int32),
            pltpu.SemaphoreType.DMA((blocks,)),
            pltpu.SemaphoreType.DMA((blocks,)),
            pltpu.SemaphoreType.DMA((4,)),
            pltpu.SemaphoreType.DMA((4,)),
            pltpu.SemaphoreType.DMA((4, 4)),
            pltpu.SemaphoreType.DMA((4, 4)),
            pltpu.SemaphoreType.DMA((2, 4)),
            pltpu.SemaphoreType.DMA((2, 4)),
            pltpu.VMEM((rows, cols), F32),
            pltpu.VMEM((1, pairs), F32),
            pltpu.VMEM((pairs, pairs), BF),
            pltpu.VMEM((excits, cols), jnp.int32),
            pltpu.VMEM((excits, cols), jnp.int32),
            pltpu.VMEM((excits, cols), jnp.int32),
            pltpu.VMEM((excits, rows), jnp.int32),
            pltpu.VMEM((excits, rows), jnp.int32),
            pltpu.VMEM((excits, rows), jnp.int32),
            pltpu.SemaphoreType.DMA((9,)),
        ],
        compiler_params=pltpu.CompilerParams(
            vmem_limit_bytes=56 * 2**20, collective_id=0, has_side_effects=True
        ),
    )(ci_vector, one_body.reshape(1, pairs), pair_integrals, bt, bp, bs, at, ap, asg)


def solution(mesh):
    placed = (
        P("alpha", "beta"),
        P(),
        P(),
        P(None, "beta"),
        P(None, "beta"),
        P(None, "beta"),
        P(None, "alpha"),
        P(None, "alpha"),
        P(None, "alpha"),
    )
    return jax.shard_map(
        shards, mesh=mesh, in_specs=placed, out_specs=P("alpha", "beta"), check_vma=False
    )
```

```python
import functools

import jax
import jax.numpy as jnp
from jax import lax
from jax.experimental import pallas as pl
from jax.experimental.pallas import tpu as pltpu
from jax.sharding import PartitionSpec as P

BF = jnp.bfloat16
F32 = jnp.float32
MESH = pl.DeviceIdType.MESH
NT = (((1,), (1,)), ((), ()))
TN = (((0,), (0,)), ((), ()))
LANES = 128
WIDE = 512
DS = 132
SS = 136
LS = 136
BATCH = 11


def iota(shape, dim):
    return lax.broadcasted_iota(jnp.int32, shape, dim)


def compute_kernel(
    hi_lane,
    *refs,
):
    given, refs = refs[:9], refs[9:]
    (
        out_ref,
        rows_ref,
        near_part_ref,
        far_part_ref,
        near_got_ref,
        far_got_ref,
        last_part_ref,
        last_got_ref,
        one_pad_ref,
        pair_pad_ref,
        code_ref,
        turned_ref,
        group_ref,
        dens_ref,
        sv_ref,
        lift_ref,
        lift_bf_ref,
        wide_ref,
        own_ref,
        even_ref,
        odd_ref,
        order_ref,
        beta_send,
        beta_recv,
        near_send,
        near_recv,
        far_send,
        far_recv,
        last_send,
        last_recv,
        ci_ref,
        one_ref,
        pair_ref,
        bt_ref,
        bp_ref,
        bs_ref,
        at_ref,
        ap_ref,
        as_ref,
        load_sem,
    ) = refs
    blocks, rows, cols = rows_ref.shape
    excits = bt_ref.shape[0]
    slots = excits + 2
    per_group = LANES // slots
    groups = group_ref.shape[0]
    me_beta = lax.axis_index("beta")
    me_alpha = lax.axis_index("alpha")

    barrier = pltpu.get_barrier_semaphore()
    chips = blocks // 2
    here, core = me_beta // 2, lax.rem(me_beta, 2)
    sibling = 2 * here + 1 - core
    right = 2 * lax.rem(here + 1, chips) + core
    left = 2 * lax.rem(here + chips - 1, chips) + core
    across = 2 * lax.rem(here + 2, chips) + core
    beta_peers = (sibling, left, right, across)
    for peer in beta_peers:
        pl.semaphore_signal(barrier, inc=1, device_id={"beta": peer}, device_id_type=MESH)
    mine, place = me_alpha // 4, lax.rem(me_alpha, 4)

    def at_far(far):
        return {"alpha": 4 * far + place}

    def at_near(near):
        return {"alpha": 4 * mine + near}

    def turned(start, r):
        return lax.rem(start + r, 4)

    for r in range(1, 4):
        for peer in (at_far(turned(mine, r)), at_near(turned(place, r))):
            pl.semaphore_signal(barrier, inc=1, device_id=peer, device_id_type=MESH)
    kept = (ci_ref, bt_ref, bp_ref, bs_ref, at_ref, ap_ref, as_ref, one_ref, pair_ref)
    order = (0, 3, 4, 5, 6, 7, 8, 1, 2)
    loads = [
        pltpu.make_async_copy(given[n], kept[k], load_sem.at[k]) for k, n in enumerate(order)
    ]
    for load in loads:
        load.start()
    loads[0].wait()
    rows_ref[me_beta] = ci_ref[...].astype(BF)
    pl.semaphore_wait(barrier, len(beta_peers) + 6)

    def row_copy(k, block, target):
        return pltpu.make_async_remote_copy(
            src_ref=rows_ref.at[block],
            dst_ref=rows_ref.at[block],
            send_sem=beta_send.at[k],
            recv_sem=beta_recv.at[k],
            device_id={"beta": target},
            device_id_type=MESH,
        )

    def other(block):
        return block + 1 - 2 * core

    sends = [
        row_copy(0, me_beta, across),
        row_copy(1, me_beta, right),
        row_copy(2, me_beta, left),
        row_copy(3, me_beta, sibling),
        row_copy(4, across, sibling),
        row_copy(5, left, sibling),
        row_copy(6, right, sibling),
    ]
    arrivals = [
        row_copy(0, across, me_beta),
        row_copy(1, left, me_beta),
        row_copy(2, right, me_beta),
        row_copy(3, sibling, me_beta),
        row_copy(4, other(across), me_beta),
        row_copy(5, other(left), me_beta),
        row_copy(6, other(right), me_beta),
    ]

    def near_copy(source, target):
        return pltpu.make_async_remote_copy(
            src_ref=near_part_ref.at[target],
            dst_ref=near_got_ref.at[source],
            send_sem=near_send.at[target],
            recv_sem=near_recv.at[source],
            device_id=at_near(target),
            device_id_type=MESH,
        )

    def far_copy(source, target, near):
        return pltpu.make_async_remote_copy(
            src_ref=far_part_ref.at[near, target],
            dst_ref=far_got_ref.at[source, near],
            send_sem=far_send.at[near, target],
            recv_sem=far_recv.at[source, near],
            device_id=at_far(target),
            device_id_type=MESH,
        )

    def near_last(source, target):
        return pltpu.make_async_remote_copy(
            src_ref=last_part_ref.at[1, target],
            dst_ref=last_got_ref.at[1, source],
            send_sem=last_send.at[1, target],
            recv_sem=last_recv.at[1, source],
            device_id=at_near(target),
            device_id_type=MESH,
        )

    def far_last(source, target):
        return pltpu.make_async_remote_copy(
            src_ref=last_part_ref.at[0, target],
            dst_ref=last_got_ref.at[0, source],
            send_sem=last_send.at[0, target],
            recv_sem=last_recv.at[0, source],
            device_id=at_far(target),
            device_id_type=MESH,
        )

    for k in range(4):
        sends[k].start()

    for load in loads[1:]:
        load.wait()

    code_ref[...] = jnp.zeros_like(code_ref)
    listed = bt_ref[...] + 2048 * bp_ref[...] + (1 << 18) * bs_ref[...]
    code_ref[0:excits, :] = listed.astype(F32)
    own = me_beta * cols + iota((8, cols), 1)
    extra = iota((8, cols), 0)
    own = jnp.where(extra < 2, own + 2048 * (hi_lane + extra) + (1 << 18), 0)
    code_ref[excits : excits + 8, :] = own.astype(F32)
    turned_ref[...] = jnp.zeros_like(turned_ref)
    turned_ref[0:cols, :] = code_ref[...].T
    grouped = turned_ref[pl.ds(0, groups, stride=per_group), :]
    for t in range(1, per_group):
        shifted = turned_ref[pl.ds(t, groups, stride=per_group), :]
        grouped = grouped + pltpu.roll(shifted, t * slots, 1)
    group_ref[...] = grouped.astype(jnp.int32)

    device = at_ref[...] // rows
    near = jnp.bitwise_and(jnp.bitwise_and(device, 3) - place + 3, 3)
    order_ref[...] = (4 * near + device // 4) * rows + jnp.bitwise_and(at_ref[...], rows - 1)

    wide = wide_ref.shape[1]
    arrivals[3].wait_recv()

    def widen(r):
        chip = 2 * turned(here, r)
        for c in range(2):
            wide_ref[r * rows : (r + 1) * rows, c * cols : (c + 1) * cols] = rows_ref[chip + c]

    def pick_code(step):
        coded = [group_ref[pl.ds(2 * step + u, 1), :] for u in range(2)]
        code = jnp.concatenate(coded, axis=1)
        target = jnp.bitwise_and(code, 2047)
        low = jnp.bitwise_and(target, wide - 1)
        sign = (2 * lax.shift_right_logical(code, 18) - 1).astype(F32)
        pick = jnp.where(iota((wide, 2 * LANES), 0) == low, sign, 0.0).astype(BF)
        return jnp.bitwise_and(target // wide - here + chips, chips - 1), pick

    def own_step(step, carry):
        unused, pick = pick_code(step)
        found = jnp.dot(wide_ref[0:rows, :], pick, preferred_element_type=F32).astype(BF)
        for u in range(2):
            own_ref[2 * step + u] = found[:, u * LANES : (u + 1) * LANES]
        return carry

    widen(0)
    lax.fori_loop(0, groups // 2, own_step, 0, unroll=4)

    for k, passed in ((1, 5), (2, 6), (0, 4)):
        arrivals[k].wait_recv()
        sends[passed].start()

    pairs = pair_ref.shape[0]
    one_pad_ref[...] = jnp.zeros_like(one_pad_ref)
    one_pad_ref[0:1, 0:pairs] = one_ref[...]
    pair_pad_ref[...] = jnp.zeros_like(pair_pad_ref)
    pair_pad_ref[0:pairs, 0:pairs] = pair_ref[...].astype(F32)
    one_row = one_pad_ref[0:1, :]
    one_hi = one_row.astype(BF).astype(F32)
    one_lo = one_row - one_hi
    one_two = jnp.concatenate([one_hi, one_lo, jnp.zeros((6, LANES), F32)], axis=0)
    one_cols = jnp.concatenate([one_two, jnp.zeros((LANES - 8, LANES), F32)], axis=0).T
    lane = iota((LANES, LANES), 1)
    table = pair_pad_ref[...]
    table = jnp.where(lane == hi_lane, one_cols[:, 0:1], table)
    table = jnp.where(lane == hi_lane + 1, one_cols[:, 1:2], table)
    table = table.astype(BF)

    def sv_step(e, carry):
        which = ap_ref[pl.ds(e, 1), :]
        sign = (2 * as_ref[pl.ds(e, 1), :] - 1).astype(F32)
        hot = jnp.where(iota((LANES, rows), 0) == which, sign, 0.0).astype(BF)
        sv = lax.dot_general(hot, table, TN, preferred_element_type=F32)
        sv_ref[pl.ds(pl.multiple_of(e * SS, 8), rows), :] = sv
        return carry

    lax.fori_loop(0, excits, sv_step, 0, unroll=8)
    for e, row in enumerate((one_hi, one_lo)):
        start = (excits + e) * SS
        sv_ref[start : start + rows, :] = jnp.broadcast_to(row, (rows, LANES))
    sv_ref[(excits + 2) * SS :, :] = jnp.zeros(((46 - excits) * SS, LANES), F32)

    for k in (5, 6, 4):
        arrivals[k].wait_recv()

    for r in range(1, chips):
        widen(r)
    lane_row = iota((1, LANES), 1)
    lane_slot = lane_row // slots

    def pick_step(step, held, slot):
        block, pick = pick_code(step)
        found = jnp.dot(wide_ref[rows:, :], pick, preferred_element_type=F32)
        picked = jnp.concatenate([own_ref[2 * step + u] for u in range(2)], axis=1).astype(F32)
        for r in range(1, chips):
            picked = jnp.where(block == r, found[(r - 1) * rows : r * rows], picked)
        picked = picked.astype(BF)
        for u in range(2):
            held[2 * slot + u] = picked[:, u * LANES : (u + 1) * LANES]

    def density_step(g, held, slot):
        code = group_ref[pl.ds(g, 1), :]
        pair = jnp.bitwise_and(lax.shift_right_logical(code, 11), 127)
        goal = jnp.where(lane_slot < per_group, lane_slot * LANES + pair, -1)
        spots = iota((per_group * LANES, LANES), 0) == goal
        hot = jnp.where(spots, 1.0, 0.0).astype(BF)
        dens = lax.dot_general(held[slot], hot, NT, preferred_element_type=F32)
        for t in range(per_group):
            base = (per_group * g + t) * DS
            dens_ref[pl.ds(pl.multiple_of(base, 4), rows), :] = dens[
                :, t * LANES : (t + 1) * LANES
            ]

    def both(j, last, held):
        for u in range(BATCH):
            if held is not None:
                pick_step(BATCH * j + u, held, u)
            if last is not None:
                for v in (2 * u, 2 * u + 1):
                    density_step(2 * BATCH * (j - 1) + v, last, v)

    def both_step(k, carry):
        both(2 * k + 1, even_ref, odd_ref)
        both(2 * k + 2, odd_ref, even_ref)
        return carry

    batches = groups // (2 * BATCH)
    both(0, None, even_ref)
    lax.fori_loop(0, (batches - 1) // 2, both_step, 0)
    if batches % 2:
        both(batches, even_ref, None)
    else:
        both(batches - 1, even_ref, odd_ref)
        both(batches, odd_ref, None)

    def lift_step(a, carry):
        weights = sv_ref[pl.ds(a, 48, stride=SS), :].astype(BF)
        dens = dens_ref[pl.ds(a, cols, stride=DS), :].astype(BF)
        out = lax.dot_general(weights, dens, NT, preferred_element_type=F32)
        for half in range(2):
            lift_ref[half, pl.ds(a, 48, stride=LS), :] = out[:, half * LANES : (half + 1) * LANES]
        return carry

    lax.fori_loop(0, rows, lift_step, 0, unroll=64)
    for half in range(2):
        at_half = slice(half * LANES, (half + 1) * LANES)
        for e in range(excits):
            lift_bf_ref[e * rows : (e + 1) * rows, at_half] = lift_ref[
                half, e * LS : e * LS + rows, :
            ].astype(BF)

    tall = 4 * rows

    def spread_step(s, carry):
        hots = []
        for e in range(excits):
            goal = order_ref[e : e + 1, :] - s * tall
            hots.append(jnp.where(iota((tall, rows), 0) == goal, 1.0, 0.0).astype(BF))
        hot = jnp.concatenate(hots, axis=1)
        out = jnp.dot(hot, lift_bf_ref[...], preferred_element_type=F32).astype(BF)
        near = turned(place, s + 1)
        for far in range(4):
            at_rows = slice(far * rows, (far + 1) * rows)
            near_part_ref[near, far] = out[at_rows, 0:LANES]
            far_part_ref[near, far] = out[at_rows, LANES : 2 * LANES]

        @pl.when(s < 3)
        def _():
            near_copy(place, near).start()

        for r in (2, 1, 3):
            far_copy(mine, turned(mine, r), near).start()
        return carry

    lax.fori_loop(0, 4, spread_step, 0)

    for half in range(2):
        at_half = slice(half * LANES, (half + 1) * LANES)
        out_ref[:, at_half] = (
            lift_ref[half, excits * LS : excits * LS + rows, :]
            + lift_ref[half, (excits + 1) * LS : (excits + 1) * LS + rows, :]
        )

    for r in range(1, 4):
        near_copy(turned(place, r), place).wait_recv()
    for r in (2, 1, 3, 0):
        far = turned(mine, r)
        total = near_part_ref[place, far].astype(F32)
        for q in range(1, 4):
            total = total + near_got_ref[turned(place, q), far].astype(F32)
        if r:
            last_part_ref[0, far] = total.astype(BF)
            far_last(mine, far).start()
        else:
            out_ref[:, 0:LANES] = out_ref[:, 0:LANES] + total

    for r in (2, 1, 3, 0):
        near = turned(place, r)
        total = far_part_ref[near, mine].astype(F32)
        for q in range(1, 4):
            source = turned(mine, q)
            far_copy(source, mine, near).wait_recv()
            total = total + far_got_ref[source, near].astype(F32)
        if r:
            last_part_ref[1, near] = total.astype(BF)
            near_last(place, near).start()
        else:
            out_ref[:, LANES : 2 * LANES] = out_ref[:, LANES : 2 * LANES] + total

    total = out_ref[:, 0:LANES]
    for r in range(1, 4):
        far_last(turned(mine, r), mine).wait_recv()
        total = total + last_got_ref[0, turned(mine, r)].astype(F32)
    out_ref[:, 0:LANES] = total
    total = out_ref[:, LANES : 2 * LANES]
    for r in range(1, 4):
        near_last(turned(place, r), place).wait_recv()
        total = total + last_got_ref[1, turned(place, r)].astype(F32)
    out_ref[:, LANES : 2 * LANES] = total

    for copy in sends:
        copy.wait_send()
    for r in range(1, 4):
        near_copy(place, turned(place, r)).wait_send()
        far_last(mine, turned(mine, r)).wait_send()
        near_last(place, turned(place, r)).wait_send()
        for near in range(4):
            far_copy(mine, turned(mine, r), near).wait_send()


def shards(ci_vector, one_body, pair_integrals, bt, bp, bs, at, ap, asg):
    rows, cols = ci_vector.shape
    blocks = lax.axis_size("beta")
    pairs = one_body.shape[0]
    excits = bt.shape[0]
    per_group = LANES // (excits + 2)
    used = -(-cols // per_group)
    groups = -(-used // (2 * BATCH)) * 2 * BATCH
    vmem = pl.BlockSpec(memory_space=pltpu.VMEM)
    return pl.pallas_call(
        functools.partial(compute_kernel, pairs),
        out_shape=jax.ShapeDtypeStruct((rows, cols), F32),
        in_specs=[pl.BlockSpec(memory_space=pltpu.HBM)] * 9,
        out_specs=vmem,
        scratch_shapes=[
            pltpu.VMEM((blocks, rows, cols), BF),
            pltpu.VMEM((4, 4, rows, LANES), BF),
            pltpu.VMEM((4, 4, rows, LANES), BF),
            pltpu.VMEM((4, 4, rows, LANES), BF),
            pltpu.VMEM((4, 4, rows, LANES), BF),
            pltpu.VMEM((2, 4, rows, LANES), BF),
            pltpu.VMEM((2, 4, rows, LANES), BF),
            pltpu.VMEM((8, LANES), F32),
            pltpu.VMEM((LANES, LANES), F32),
            pltpu.VMEM((LANES, cols), F32),
            pltpu.VMEM((groups * per_group, LANES), F32),
            pltpu.VMEM((groups, LANES), jnp.int32),
            pltpu.VMEM((groups * per_group * DS, LANES), F32),
            pltpu.VMEM((48 * SS, LANES), F32),
            pltpu.VMEM((2, 48 * LS, LANES), F32),
            pltpu.VMEM((excits * rows, cols), BF),
            pltpu.VMEM((blocks * rows * cols // WIDE, WIDE), BF),
            pltpu.VMEM((groups, rows, LANES), BF),
            pltpu.VMEM((2 * BATCH, rows, LANES), BF),
            pltpu.VMEM((2 * BATCH, rows, LANES), BF),
            pltpu.VMEM((excits, rows), jnp.int32),
            pltpu.SemaphoreType.DMA((blocks,)),
            pltpu.SemaphoreType.DMA((blocks,)),
            pltpu.SemaphoreType.DMA((4,)),
            pltpu.SemaphoreType.DMA((4,)),
            pltpu.SemaphoreType.DMA((4, 4)),
            pltpu.SemaphoreType.DMA((4, 4)),
            pltpu.SemaphoreType.DMA((2, 4)),
            pltpu.SemaphoreType.DMA((2, 4)),
            pltpu.VMEM((rows, cols), F32),
            pltpu.VMEM((1, pairs), F32),
            pltpu.VMEM((pairs, pairs), BF),
            pltpu.VMEM((excits, cols), jnp.int32),
            pltpu.VMEM((excits, cols), jnp.int32),
            pltpu.VMEM((excits, cols), jnp.int32),
            pltpu.VMEM((excits, rows), jnp.int32),
            pltpu.VMEM((excits, rows), jnp.int32),
            pltpu.VMEM((excits, rows), jnp.int32),
            pltpu.SemaphoreType.DMA((9,)),
        ],
        compiler_params=pltpu.CompilerParams(
            vmem_limit_bytes=56 * 2**20, collective_id=0, has_side_effects=True
        ),
    )(ci_vector, one_body.reshape(1, pairs), pair_integrals, bt, bp, bs, at, ap, asg)


def solution(mesh):
    placed = (
        P("alpha", "beta"),
        P(),
        P(),
        P(None, "beta"),
        P(None, "beta"),
        P(None, "beta"),
        P(None, "alpha"),
        P(None, "alpha"),
        P(None, "alpha"),
    )
    return jax.shard_map(
        shards, mesh=mesh, in_specs=placed, out_specs=P("alpha", "beta"), check_vma=False
    )
```
